32 devices in a mesh: group: 2 (over y), dev: 8 (over z, x), tp: 2 (over core).
Axes of the slice: x: 2, y: 2, z: 4, core: 2. Of those that a mesh axis runs over, the one named last changes fastest.
Arguments:
- prompt_activations: bfloat16 [4096, 8192], P(('group', 'dev')), parts along dimension 0, may hold values from -6 to 6
- key_matrix: bfloat16 [8192, 512], P('dev', 'tp'), may hold values from -0.0625 to 0.0625
- value_matrix: bfloat16 [8192, 512], P('dev', 'tp'), may hold values from -0.0625 to 0.0625
- adapter_down_keyvalue: bfloat16 [8192, 128], P('dev'), may hold values from -0.0625 to 0.0625
- adapter_up_key: bfloat16 [64, 512], P(None, 'tp'), may hold values from -1.5 to 1.5
- adapter_up_value: bfloat16 [64, 512], P(None, 'tp'), may hold values from -1.5 to 1.5
- request_adapter: int32 [16], P('group'), parts along dimension 0, may hold values from 0 to 3
- page_request: int32 [1024, 1], P('group'), parts along dimension 0, may hold values from 0 to 7; in each aligned block of 64 rows (0 to 63, 64 to 127, ...) at most 8 rows name the same one
- context_tokens: int32 [16], P('group'), parts along dimension 0, may hold values from 64 to 256
- step_query: bfloat16 [16, 4096], P(('group', 'dev'), 'tp'), parts along dimension 0, may hold values from -256 to 256
- step_key: bfloat16 [16, 512], P(('group', 'dev'), 'tp'), parts along dimension 0, may hold values from -6 to 6
- step_value: bfloat16 [16, 512], P(('group', 'dev'), 'tp'), parts along dimension 0, may hold values from -6 to 6
- stored_keys: bfloat16 [16, 256, 512], P(('group', 'dev'), None, 'tp'), parts along dimension 0, may hold values from -6 to 6
- stored_values: bfloat16 [16, 256, 512], P(('group', 'dev'), None, 'tp'), parts along dimension 0, may hold values from -6 to 6
- output_matrix: bfloat16 [4096, 8192], P('tp', 'dev'), may hold values from -0.09375 to 0.09375
- adapter_down_output: bfloat16 [4096, 64], P('tp'), may hold values from -0.09375 to 0.09375
- adapter_up_output: bfloat16 [64, 8192], P(None, 'dev'), may hold values from -1.5 to 1.5
Outputs:
- attended: bfloat16 [16, 8192], P('group', 'dev'), parts along dimension 0
The draws below stay inside these ranges and needn't reach their ends.
There are 2 independent parts, one for each index of `group`. The reference program is written for one: setup_inputs(seed, part) draws one part's arguments, and reference() takes and returns one part's arrays. A program takes and returns all parts, laid end to end along the dimension named above; an argument that names none is the same for every part. Nothing has to cross between parts.
Inputs may be any that keep to these rules, and one draw needn't show every extreme that they name: `page_request`: among the pages of one device's prompt block (aligned blocks of 64 pages), no request owns more than 8; every request owns at least one page.
All inputs are finite; a program needn't handle non-finite values.
Results may differ from the reference program's by a relative error of at most 0.0086.
Values may be sent and summed in bfloat16 or wider, within the bound.
A program may use at most 64 MiB of HBM per device.

```python
import math
import jax
import jax.numpy as jnp
import numpy as np
from jax import lax

MODEL_WIDTH = 8192
HEADS = 32
KV_HEADS = 4
HEAD = 128
LOW_RANK = 16
ADAPTER_COUNT = 4
TOK_DEV = 256
PAGE = 4
CTX = 256
CAP = 8
QUERY_WIDTH = 4096
KEY_WIDTH = 512
ROWS = 8
TOKENS = 2048
PAGES = 512
N_DEV = 8


def drawn_draw(key):
    base_key = jax.random.fold_in(jax.random.fold_in(key, 7), 3)
    base_keys = jnp.clip(jax.random.normal(base_key, (ROWS, CTX, KEY_WIDTH), jnp.float32), -6.0, 6.0)
    return base_keys


def draw_stored_keys(key, part):
    base_keys = drawn_draw(key)
    return base_keys.astype(jnp.bfloat16)


def draw_step_query(key, part):
    normal_part = jnp.clip(2.0 * jax.random.normal(jax.random.fold_in(key, 11), (ROWS, QUERY_WIDTH), jnp.float32), -12.0, 12.0)
    return normal_part.astype(jnp.bfloat16)


def with_ends(array, key, smallest, top_value):
    spot = [jax.random.randint(jax.random.fold_in(key, axis), (), 0, length) for axis, length in enumerate(array.shape)]
    longest = array.shape.index(max(array.shape))
    neighbour = spot[:longest] + [(spot[longest] + 1) % array.shape[longest]] + spot[longest + 1:]
    return array.at[tuple(spot)].set(smallest).at[tuple(neighbour)].set(top_value)


def block_levels(own_key, dims, cuts, low, largest):
    level, own = 1.0, jax.random.fold_in(own_key, 6)
    for axis_at, parts in cuts:
        draws = jnp.exp(jax.random.uniform(jax.random.fold_in(own, axis_at), (parts,), jnp.float32, low / len(cuts), largest / len(cuts)))
        level = level * jnp.repeat(draws, dims[axis_at] // parts).reshape([-1 if axis == axis_at else 1 for axis in range(len(dims))])
    return level


def assign_block(key, own, number, rows, amount, top, bound, skew):
    order = jax.random.permutation(key, amount)
    heavy_load, usual = portions_of(amount, rows * top, bound, skew, True), portions_of(amount, rows * top, bound, skew, False)
    places = jnp.arange(amount)

    def named(tallies, offset_by):
        used = int((tallies > 0).sum())
        fixed = max(1, used // 4)
        passed = fixed + (places - fixed + offset_by * (used - fixed)) % max(1, amount - fixed)
        return jnp.zeros((amount,), jnp.int32).at[order[jnp.where(places < fixed, places, passed)]].set(jnp.asarray(tallies, jnp.int32))

    tallies = jnp.where(number % 4 == 0, named(heavy_load, number // 4), named(usual, number - number // 4 - 1))
    mixed = jax.random.permutation(jax.random.fold_in(own, 3), amount)
    donor, receiver = mixed[0:amount // 2 * 2:2], mixed[1:amount // 2 * 2:2]
    room = jnp.minimum(tallies[donor] - 1, bound - tallies[receiver]) // 2
    room = jnp.where((donor == order[0]) | (receiver == order[0]) | (tallies[receiver] == 0), 0, jnp.maximum(room, 0))
    passed = jax.random.randint(jax.random.fold_in(own, 4), (amount // 2,), 0, 1 << 20) % (room + 1)
    tallies = tallies.at[donor].add(-passed).at[receiver].add(passed)
    members = jnp.searchsorted(jnp.cumsum(tallies), jnp.arange(rows * top), side="right").astype(jnp.int32)
    grid = members.reshape(top, rows).T
    grid = grid[jax.random.permutation(jax.random.fold_in(own, 1), rows)]
    offset_by = jax.random.randint(jax.random.fold_in(own, 2), (rows, 1), 0, top)
    return jnp.take_along_axis(grid, (jnp.arange(top)[None, :] + offset_by) % top, axis=1)


def portions_of(count, total, bound, lean, full):
    loads = [(1 << 20) // math.isqrt(standing ** lean) + 1 for standing in range(1, count + 1)]
    largest = bound if full else min(bound, max(-(-total // count), total * loads[0] // sum(loads)))
    least = 1 if total - largest >= count - 1 else 0
    given, spare = [largest] + [least] * (count - 1), total - largest - least * (count - 1)
    while spare > 0:
        candidates = [i for i in range(1, count) if given[i] < largest] or [i for i in range(1, count) if given[i] < bound]
        pool, remaining = sum([loads[i] for i in candidates]), spare
        for i in candidates:
            more = min(bound - given[i], max(1, remaining * loads[i] // pool), spare)
            given[i] = given[i] + more
            spare = spare - more
    return np.array(given)


def normal_values(rng, dims, scale, most, shards=(), kind=jnp.bfloat16):
    level = block_levels(rng, dims, shards, -0.22, 0.18) if shards else 1.0
    result = jax.random.normal(rng, dims, jnp.float32) * scale * level
    return jnp.minimum(jnp.maximum(result, -most), most).astype(kind)


def setup_inputs(seed: int = 0, part: int = 0) -> dict:
    splits = jax.random.split(jax.random.key(seed), 18)
    own_keys = jax.random.split(jax.random.fold_in(splits[17], part), 18)
    prompt_activations = normal_values(own_keys[0], (TOKENS, MODEL_WIDTH), 1.0, 6.0, ((0, 8),))
    key_matrix = normal_values(splits[1], (MODEL_WIDTH, KEY_WIDTH), MODEL_WIDTH ** -0.5, 0.0625, ((0, 8), (1, 2)))
    value_matrix = normal_values(splits[2], (MODEL_WIDTH, KEY_WIDTH), MODEL_WIDTH ** -0.5, 0.0625, ((0, 8), (1, 2)))
    adapter_down_keyvalue = normal_values(splits[3], (MODEL_WIDTH, 2 * ADAPTER_COUNT * LOW_RANK), MODEL_WIDTH ** -0.5, 0.0625, ((0, 8),))
    adapter_up_key = normal_values(splits[4], (ADAPTER_COUNT * LOW_RANK, KEY_WIDTH), LOW_RANK ** -0.5, 1.5, ((1, 2),))
    adapter_up_value = normal_values(splits[5], (ADAPTER_COUNT * LOW_RANK, KEY_WIDTH), LOW_RANK ** -0.5, 1.5, ((1, 2),))
    request_adapter = with_ends(jax.random.randint(own_keys[6], (ROWS,), 0, ADAPTER_COUNT), jax.random.fold_in(own_keys[6], 1), 0, ADAPTER_COUNT - 1).astype(jnp.int32)
    page_request_keys = jax.random.split(jax.random.fold_in(own_keys[7], 1), PAGES // (TOK_DEV // PAGE))
    page_request_turns = jax.random.permutation(jax.random.fold_in(own_keys[7], 3), PAGES // (TOK_DEV // PAGE))
    page_request = jax.vmap(lambda own, number: assign_block(jax.random.fold_in(own_keys[7], 2), own, number, TOK_DEV // PAGE, ROWS, 1, CAP, 2))(page_request_keys, page_request_turns).reshape((PAGES, 1))
    context_tokens = with_ends(jax.random.randint(own_keys[8], (ROWS,), CTX // 4, CTX + 1), jax.random.fold_in(own_keys[8], 1), CTX // 4, CTX).astype(jnp.int32)
    step_query = draw_step_query(jax.random.fold_in(jax.random.fold_in(splits[17], part), 71), part)
    step_key = normal_values(own_keys[10], (ROWS, KEY_WIDTH), 1.0, 6.0, ((0, 8), (1, 2)))
    step_value = normal_values(own_keys[11], (ROWS, KEY_WIDTH), 1.0, 6.0, ((0, 8), (1, 2)))
    stored_keys = draw_stored_keys(jax.random.fold_in(jax.random.fold_in(splits[17], part), 71), part)
    stored_values = normal_values(own_keys[13], (ROWS, CTX, KEY_WIDTH), 1.0, 6.0, ((0, 8), (2, 2)))
    output_matrix = normal_values(splits[14], (QUERY_WIDTH, MODEL_WIDTH), QUERY_WIDTH ** -0.5, 0.09375, ((0, 2), (1, 8)))
    adapter_down_output = normal_values(splits[15], (QUERY_WIDTH, ADAPTER_COUNT * LOW_RANK), QUERY_WIDTH ** -0.5, 0.09375, ((0, 2),))
    adapter_up_output = normal_values(splits[16], (ADAPTER_COUNT * LOW_RANK, MODEL_WIDTH), LOW_RANK ** -0.5, 1.5, ((1, 8),))
    return dict(prompt_activations=prompt_activations, key_matrix=key_matrix, value_matrix=value_matrix, adapter_down_keyvalue=adapter_down_keyvalue, adapter_up_key=adapter_up_key, adapter_up_value=adapter_up_value, request_adapter=request_adapter, page_request=page_request, context_tokens=context_tokens, step_query=step_query, step_key=step_key, step_value=step_value, stored_keys=stored_keys, stored_values=stored_values, output_matrix=output_matrix, adapter_down_output=adapter_down_output, adapter_up_output=adapter_up_output)


adapter_scale = 1.0
rope_base = 500000.0


def rotate(key_rows, positions):
    row_count = key_rows.shape[0]
    blocks = key_rows.reshape(row_count, -1, HEAD)
    half_size = HEAD // 2
    exponent = jnp.arange(half_size, dtype=jnp.float32) * (2.0 / HEAD)
    frequency = jnp.exp(-jnp.log(jnp.float32(rope_base)) * exponent)
    angles = positions.astype(jnp.float32)[:, None] * frequency[None, :]
    cosine = jnp.cos(angles)[:, None, :]
    sine_part = jnp.sin(angles)[:, None, :]
    first_half = blocks[..., :half_size]
    second_half = blocks[..., half_size:]
    turned = jnp.concatenate([first_half * cosine - second_half * sine_part, second_half * cosine + first_half * sine_part], axis=-1)
    return turned.reshape(row_count, -1)


def owner_ranks(owners, row_total):
    onehot = (owners[:, None] == jnp.arange(row_total, dtype=jnp.int32)[None, :]).astype(jnp.int32)
    before = jnp.cumsum(onehot, axis=0) - onehot
    rank = jnp.sum(before * onehot, axis=1).astype(jnp.int32)
    return onehot, rank


def mask_columns(narrowed, adapter_list):
    column = jnp.arange(narrowed.shape[1], dtype=jnp.int32)
    owner = (column % (ADAPTER_COUNT * LOW_RANK)) // LOW_RANK
    return jnp.where(owner[None, :] == adapter_list[:, None], narrowed, jnp.zeros_like(narrowed))


def selected_narrow(activation_rows, adapter_down, adapter_list):
    narrowed = jnp.dot(activation_rows, adapter_down, preferred_element_type=jnp.float32)
    return mask_columns(narrowed, adapter_list)


def widened(selected_rows, up_key, up_value):
    split_at = ADAPTER_COUNT * LOW_RANK
    highest = lax.Precision.HIGHEST
    key_portion = jnp.dot(selected_rows[:, :split_at], up_key.astype(jnp.float32), precision=highest)
    value_portion = jnp.dot(selected_rows[:, split_at:], up_value.astype(jnp.float32), precision=highest)
    return adapter_scale * key_portion, adapter_scale * value_portion


def attend(query, old_keys, old_values, old_length, fresh_keys, fresh_values, fresh_valid, last_key, last_value):
    all_keys = jnp.concatenate([old_keys, fresh_keys, last_key[None, :]], axis=0).astype(jnp.float32)
    all_values = jnp.concatenate([old_values, fresh_values, last_value[None, :]], axis=0).astype(jnp.float32)
    old_valid = jnp.arange(old_keys.shape[0], dtype=jnp.int32) < old_length
    valid = jnp.concatenate([old_valid, fresh_valid, jnp.ones((1,), dtype=bool)])
    group_size = HEADS // KV_HEADS
    query_heads = query.astype(jnp.float32).reshape(-1, group_size, HEAD)
    key_count = all_keys.shape[0]
    key_heads = all_keys.reshape(key_count, -1, HEAD)
    value_heads = all_values.reshape(key_count, -1, HEAD)
    scores = jnp.einsum("kgd,lkd->kgl", query_heads, key_heads) * (HEAD ** -0.5)
    scores = jnp.where(valid[None, None, :], scores, -1e30)
    top = jnp.max(scores, axis=-1, keepdims=True)
    weights = jnp.exp(scores - top)
    total = jnp.sum(weights, axis=-1, keepdims=True)
    probs = (weights / total).astype(jnp.bfloat16)
    output = jnp.einsum("kgl,lkd->kgd", probs.astype(jnp.float32), value_heads)
    return output.reshape(-1).astype(jnp.bfloat16)


def reference(prompt_activations, key_matrix, value_matrix, adapter_down_keyvalue, adapter_up_key, adapter_up_value, request_adapter, page_request, context_tokens, step_query, step_key, step_value, stored_keys, stored_values, output_matrix, adapter_down_output, adapter_up_output):
    token_total = prompt_activations.shape[0]
    owners = page_request[:, 0].astype(jnp.int32)
    pages_total = owners.shape[0]
    onehot, rank = owner_ranks(owners, ROWS)
    tokens = jnp.arange(token_total, dtype=jnp.int32)
    token_page = tokens // PAGE
    token_row = jnp.take(owners, token_page)
    position = (jnp.take(context_tokens, token_row) + jnp.take(rank, token_page) * PAGE + tokens % PAGE).astype(jnp.int32)
    adapter_list = jnp.take(request_adapter, token_row).astype(jnp.int32)
    selected_rows = selected_narrow(prompt_activations, adapter_down_keyvalue, adapter_list)
    key_delta, value_delta = widened(selected_rows, adapter_up_key, adapter_up_value)
    key_raw = jnp.dot(prompt_activations, key_matrix, preferred_element_type=jnp.float32) + key_delta
    value_raw = jnp.dot(prompt_activations, value_matrix, preferred_element_type=jnp.float32) + value_delta
    new_keys = rotate(key_raw, position).astype(jnp.bfloat16)
    new_values = value_raw.astype(jnp.bfloat16)
    list_width = N_DEV * CAP
    table = jnp.zeros((ROWS * list_width,), jnp.int32).at[owners * list_width + rank].set(jnp.arange(pages_total, dtype=jnp.int32))
    counts = jnp.sum(onehot, axis=0).astype(jnp.int32)
    slot = jnp.arange(list_width * PAGE, dtype=jnp.int32)

    def attend_row(row):
        page_list = lax.dynamic_slice_in_dim(table, (row * list_width).astype(jnp.int32), list_width, 0)
        token_index = (jnp.take(page_list, slot // PAGE) * PAGE + slot % PAGE).astype(jnp.int32)
        fresh_keys = jnp.take(new_keys, token_index, axis=0)
        fresh_values = jnp.take(new_values, token_index, axis=0)
        fresh_valid = slot < jnp.take(counts, row) * PAGE
        return attend(step_query[row], stored_keys[row], stored_values[row], jnp.take(context_tokens, row), fresh_keys, fresh_values, fresh_valid, step_key[row], step_value[row])

    blended = lax.map(attend_row, jnp.arange(ROWS, dtype=jnp.int32))
    plain_result = jnp.dot(blended, output_matrix, preferred_element_type=jnp.float32)
    selected_output = selected_narrow(blended, adapter_down_output, request_adapter)
    adapter_delta = adapter_scale * jnp.dot(selected_output, adapter_up_output.astype(jnp.float32), precision=lax.Precision.HIGHEST)
    return (plain_result + adapter_delta).astype(jnp.bfloat16)
```

```python
import functools

import jax
import jax.numpy as jnp
from jax import lax
from jax.experimental import pallas as pl
from jax.experimental.pallas import tpu as pltpu
from jax.sharding import PartitionSpec as P

HEADS = 32
KV_HEADS = 4
HEAD = 128
LOW_RANK = 16
ADAPTER_COUNT = 4
PAGE = 4


adapter_scale = 1.0
rope_base = 500000.0


def rotate(key_rows, positions):
    row_count = key_rows.shape[0]
    blocks = key_rows.reshape(row_count, -1, HEAD)
    half_size = HEAD // 2
    exponent = jnp.arange(half_size, dtype=jnp.float32) * (2.0 / HEAD)
    frequency = jnp.exp(-jnp.log(jnp.float32(rope_base)) * exponent)
    angles = positions.astype(jnp.float32)[:, None] * frequency[None, :]
    cosine = jnp.cos(angles)[:, None, :]
    sine_part = jnp.sin(angles)[:, None, :]
    first_half = blocks[..., :half_size]
    second_half = blocks[..., half_size:]
    turned = jnp.concatenate(
        [
            first_half * cosine - second_half * sine_part,
            second_half * cosine + first_half * sine_part,
        ],
        axis=-1,
    )
    return turned.reshape(row_count, -1)


def owner_ranks(owners, row_total):
    onehot = (owners[:, None] == jnp.arange(row_total, dtype=jnp.int32)[None, :]).astype(jnp.int32)
    before = jnp.cumsum(onehot, axis=0) - onehot
    rank = jnp.sum(before * onehot, axis=1)
    return (onehot, rank)


def mask_columns(narrowed, adapter_list):
    column = jnp.arange(narrowed.shape[1], dtype=jnp.int32)
    owner = column % (ADAPTER_COUNT * LOW_RANK) // LOW_RANK
    return jnp.where(owner[None, :] == adapter_list[:, None], narrowed, jnp.zeros_like(narrowed))


def selected_narrow(activation_rows, adapter_down, adapter_list):
    narrowed = jnp.dot(activation_rows, adapter_down, preferred_element_type=jnp.float32)
    return mask_columns(narrowed, adapter_list)


def widened(selected_rows, up_key, up_value):
    split_at = ADAPTER_COUNT * LOW_RANK
    highest = lax.Precision.HIGHEST
    key_portion = jnp.dot(
        selected_rows[:, :split_at], up_key.astype(jnp.float32), precision=highest
    )
    value_portion = jnp.dot(
        selected_rows[:, split_at:], up_value.astype(jnp.float32), precision=highest
    )
    return (adapter_scale * key_portion, adapter_scale * value_portion)


def attend_local(
    query,
    old_keys,
    old_values,
    old_length,
    fresh_keys,
    fresh_values,
    fresh_valid,
    last_key,
    last_value,
):
    group_size = HEADS // KV_HEADS
    query_heads = query.reshape(-1, group_size, HEAD)
    kv_local = query_heads.shape[0]
    scale_factor = HEAD ** (-0.5)

    def score_of(key_rows):
        shaped = key_rows.reshape(key_rows.shape[0], kv_local, HEAD)
        return (
            jnp.einsum("kgd,lkd->kgl", query_heads, shaped, preferred_element_type=jnp.float32)
            * scale_factor
        )

    def mix_with(probs, value_rows):
        shaped = value_rows.reshape(value_rows.shape[0], kv_local, HEAD)
        return jnp.einsum("kgl,lkd->kgd", probs, shaped, preferred_element_type=jnp.float32)

    old_valid = jnp.arange(old_keys.shape[0], dtype=jnp.int32) < old_length
    old_scores = jnp.where(old_valid[None, None, :], score_of(old_keys), -1e30)
    fresh_scores = jnp.where(fresh_valid[None, None, :], score_of(fresh_keys), -1e30)
    last_score = score_of(last_key[None, :])
    top = jnp.maximum(
        jnp.maximum(
            jnp.max(old_scores, axis=-1, keepdims=True),
            jnp.max(fresh_scores, axis=-1, keepdims=True),
        ),
        last_score,
    )
    old_weights = jnp.exp(old_scores - top)
    fresh_weights = jnp.exp(fresh_scores - top)
    last_weight = jnp.exp(last_score - top)
    total = (
        jnp.sum(old_weights, axis=-1, keepdims=True)
        + jnp.sum(fresh_weights, axis=-1, keepdims=True)
        + last_weight
    )
    output = mix_with((old_weights / total).astype(jnp.bfloat16), old_values)
    output = output + mix_with((fresh_weights / total).astype(jnp.bfloat16), fresh_values)
    output = output + mix_with((last_weight / total).astype(jnp.bfloat16), last_value[None, :])
    return output.reshape(-1).astype(jnp.bfloat16)


def per_device(
    prompt_activations,
    key_matrix,
    value_matrix,
    adapter_down_keyvalue,
    adapter_up_key,
    adapter_up_value,
    request_adapter,
    page_request,
    context_tokens,
    step_query,
    step_key,
    step_value,
    stored_keys,
    stored_values,
    output_matrix,
    adapter_down_output,
    adapter_up_output,
):
    devices = lax.axis_size("dev")
    device = lax.axis_index("dev")
    tok_count = prompt_activations.shape[0]
    pages_here = tok_count // PAGE
    capacity = max(2, (pages_here + devices - 1) // devices)
    row_total = request_adapter.shape[0]
    owners = page_request[:, 0]
    onehot, rank = owner_ranks(owners, row_total)
    first_page = device * pages_here
    my_owners = lax.dynamic_slice_in_dim(owners, first_page, pages_here, 0)
    my_rank = lax.dynamic_slice_in_dim(rank, first_page, pages_here, 0)
    tokens = jnp.arange(tok_count, dtype=jnp.int32)
    token_page = tokens // PAGE
    token_owner = jnp.take(my_owners, token_page)
    position = (
        jnp.take(context_tokens, token_owner) + jnp.take(my_rank, token_page) * PAGE + tokens % PAGE
    )
    adapter_list = jnp.take(request_adapter, token_owner)
    key_width = key_matrix.shape[1]

    def add_rows(portion):
        return jnp.dot(prompt_activations, portion, preferred_element_type=jnp.float32)

    key_raw = add_rows(lax.all_gather(key_matrix, "dev", axis=0, tiled=True))
    value_raw = add_rows(lax.all_gather(value_matrix, "dev", axis=0, tiled=True))
    down_complete = lax.all_gather(adapter_down_keyvalue, "dev", axis=0, tiled=True)
    narrowed = jnp.dot(prompt_activations, down_complete, preferred_element_type=jnp.float32)
    selected_rows = mask_columns(narrowed, adapter_list)
    key_delta, value_delta = widened(selected_rows, adapter_up_key, adapter_up_value)
    key_rows = rotate(key_raw + key_delta, position).astype(jnp.bfloat16)
    value_rows = (value_raw + value_delta).astype(jnp.bfloat16)
    joined_rows = jnp.concatenate([key_rows, value_rows], axis=1)
    local_hot = (my_owners[:, None] == jnp.arange(row_total, dtype=jnp.int32)[None, :]).astype(
        jnp.int32
    )
    local_before = jnp.cumsum(local_hot, axis=0) - local_hot
    local_slot = jnp.sum(local_before * local_hot, axis=1)
    peer_slots = capacity * PAGE
    target = token_owner * peer_slots + jnp.take(local_slot, token_page) * PAGE + tokens % PAGE
    outgoing = (
        jnp.zeros((devices * peer_slots, 2 * key_width), jnp.bfloat16).at[target].set(joined_rows)
    )
    outgoing = outgoing.reshape(devices, peer_slots, 2 * key_width)
    incoming = lax.all_to_all(outgoing, "dev", split_axis=0, concat_axis=0, tiled=True)
    fresh_keys = incoming[:, :, :key_width].reshape(-1, key_width)
    fresh_values = incoming[:, :, key_width:].reshape(-1, key_width)
    my_column = jnp.take(onehot, device, axis=1)
    count_from = jnp.sum(my_column.reshape(devices, pages_here), axis=1)
    slot_page = jnp.arange(peer_slots, dtype=jnp.int32) // PAGE
    fresh_valid = (slot_page[None, :] < count_from[:, None]).reshape(-1)
    mixed_local = attend_local(
        step_query[0],
        stored_keys[0],
        stored_values[0],
        jnp.take(context_tokens, device),
        fresh_keys,
        fresh_values,
        fresh_valid,
        step_key[0],
        step_value[0],
    ).reshape(1, -1)
    portion = lax.all_gather(mixed_local, "dev", axis=0, tiled=True)
    plain_result = jnp.dot(portion, output_matrix, preferred_element_type=jnp.float32)
    selected_output = selected_narrow(portion, adapter_down_output, request_adapter)
    partial_output = plain_result + adapter_scale * jnp.dot(
        selected_output, adapter_up_output.astype(jnp.float32), precision=lax.Precision.HIGHEST
    )
    return lax.psum(partial_output, "tp").astype(jnp.bfloat16)


def iota(shape, axis):
    return lax.broadcasted_iota(jnp.int32, shape, axis)


def dot32(a, b):
    return jnp.dot(a, b, preferred_element_type=jnp.float32)


def dot_rows(a, b):
    return lax.dot_general(a, b, (((1,), (1,)), ((), ())), preferred_element_type=jnp.float32)


def halves(value):
    high = value.astype(jnp.bfloat16)
    return high, (value - high.astype(jnp.float32)).astype(jnp.bfloat16)


def fused_kernel(
    devices,
    side,
    capacity,
    x_hbm,
    wk_hbm,
    wv_hbm,
    ad_hbm,
    upk_ref,
    upv_ref,
    adapter_ref,
    owner_ref,
    context_ref,
    query_ref,
    lastk_ref,
    lastv_ref,
    oldk_hbm,
    oldv_hbm,
    wo_hbm,
    ado_hbm,
    auo_hbm,
    out_ref,
    xr,
    wcat,
    upcat,
    token_owner,
    sent,
    got,
    oldk,
    oldv,
    wo,
    ado,
    auo,
    mixes,
    part,
    other,
    local_sem,
    xs_sem,
    xr_sem,
    fs_sem,
    fr_sem,
    ps_sem,
    pr_sem,
    ms_sem,
    mr_sem,
    ts_sem,
    tr_sem,
):
    group = lax.axis_index("group")
    me = lax.axis_index("dev")
    core = lax.axis_index("tp")
    partner = (group, me, 1 - core)
    rows = owner_ref.shape[0]
    tok = x_hbm.shape[0]
    depth = wk_hbm.shape[0]
    width = wk_hbm.shape[1]
    low = ad_hbm.shape[1]
    half = tok // 2
    slots = capacity * PAGE
    outer = devices // side
    mz, mx = me // side, me % side

    def ahead(k):
        return ((mz + k // side) % outer) * side + (mx + k % side) % side

    def behind(k):
        return ((mz + outer - k // side) % outer) * side + (mx + side - k % side) % side

    own_half = pl.ds(pl.multiple_of(core * half, half), half)

    locals_ = [
        pltpu.make_async_copy(
            x_hbm.at[:, pl.ds(pl.multiple_of(me * depth, depth), depth)], xr.at[0], local_sem.at[0]
        ),
        pltpu.make_async_copy(wk_hbm, wcat.at[:, pl.ds(0, width)], local_sem.at[1]),
        pltpu.make_async_copy(wv_hbm, wcat.at[:, pl.ds(width, width)], local_sem.at[2]),
        pltpu.make_async_copy(ad_hbm, wcat.at[:, pl.ds(2 * width, low)], local_sem.at[3]),
        pltpu.make_async_copy(oldk_hbm, oldk, local_sem.at[4]),
        pltpu.make_async_copy(oldv_hbm, oldv, local_sem.at[5]),
        pltpu.make_async_copy(wo_hbm, wo, local_sem.at[6]),
        pltpu.make_async_copy(ado_hbm, ado, local_sem.at[7]),
        pltpu.make_async_copy(auo_hbm, auo, local_sem.at[8]),
    ]
    for copy in locals_[:4]:
        copy.start()

    barrier = pltpu.get_barrier_semaphore()
    for k in range(1, devices):
        pl.semaphore_signal(
            barrier, inc=1, device_id=(group, ahead(k), core), device_id_type=pl.DeviceIdType.MESH
        )
    pl.semaphore_signal(barrier, inc=1, device_id=partner, device_id_type=pl.DeviceIdType.MESH)
    pl.semaphore_wait(barrier, devices)

    def x_copy(k):
        peer = ahead(k)
        return pltpu.make_async_remote_copy(
            src_ref=x_hbm.at[own_half, pl.ds(pl.multiple_of(peer * depth, depth), depth)],
            dst_ref=xr.at[k, own_half],
            send_sem=xs_sem.at[k],
            recv_sem=xr_sem.at[k],
            device_id=(group, peer, core),
            device_id_type=pl.DeviceIdType.MESH,
        )

    def forward(k):
        return pltpu.make_async_remote_copy(
            src_ref=xr.at[k, own_half],
            dst_ref=xr.at[k, own_half],
            send_sem=fs_sem.at[k],
            recv_sem=fr_sem.at[k],
            device_id=partner,
            device_id_type=pl.DeviceIdType.MESH,
        )

    def part_copy(k, o):
        peer = ahead(o)
        source = behind(k)
        return pltpu.make_async_remote_copy(
            src_ref=sent.at[k, pl.ds(pl.multiple_of(peer * slots, slots), slots)],
            dst_ref=got.at[o, pl.ds(pl.multiple_of(source * slots, slots), slots)],
            send_sem=ps_sem.at[k, o],
            recv_sem=pr_sem.at[k, o],
            device_id=(group, peer, core),
            device_id_type=pl.DeviceIdType.MESH,
        )

    for k in range(1, devices):
        x_copy(k).start()
    for copy in locals_[4:]:
        copy.start()

    pages = owner_ref.shape[1]
    spread = (iota((pages, tok), 1) // PAGE == iota((pages, tok), 0)).astype(jnp.bfloat16)
    token_owner[...] = dot32(owner_ref[...].astype(jnp.float32).astype(jnp.bfloat16), spread)
    earlier = (iota((tok, tok), 0) // PAGE < iota((tok, tok), 1) // PAGE).astype(jnp.bfloat16)
    lora = low // 2
    upcat[...] = jnp.zeros_like(upcat)
    upcat[pl.ds(0, lora), pl.ds(0, width)] = upk_ref[...]
    upcat[pl.ds(lora, lora), pl.ds(width, width)] = upv_ref[...]
    adapters = adapter_ref[...].astype(jnp.float32)
    slot_rows = devices * slots
    row_adapter = jnp.sum(
        jnp.where(iota((slot_rows, devices), 0) // slots == iota((slot_rows, devices), 1), adapters, 0.0),
        axis=1,
        keepdims=True,
    )
    low_adapter = ((iota((slot_rows, low), 1) % lora) // LOW_RANK).astype(jnp.float32)
    keep_low = low_adapter == row_adapter

    for copy in locals_[:4]:
        copy.wait()

    def step(k, carry):
        @pl.when(k < devices - 1)
        def _():
            x_copy(k + 1).wait_recv()
            forward(k + 1).start()

        @pl.when(k > 0)
        def _():
            forward(k).wait_recv()

        source = behind(k)
        owners = token_owner[pl.ds(source, 1), :]
        hot = iota((devices, tok), 0).astype(jnp.float32) == owners
        hot32 = hot.astype(jnp.float32)
        before = dot32(hot32.astype(jnp.bfloat16), earlier)
        rank = jnp.sum(before * hot32, axis=0, keepdims=True)
        place = (
            owners * float(slots) + rank + (iota((1, tok), 1) % PAGE).astype(jnp.float32)
        )
        move = (iota((slot_rows, tok), 0).astype(jnp.float32) == place).astype(jnp.bfloat16)
        ordered = dot32(move, xr[k]).astype(jnp.bfloat16)
        wide = dot32(ordered, wcat[...])
        high, rest = halves(jnp.where(keep_low, wide[:, 2 * width :], 0.0))
        total = wide[:, : 2 * width] + dot32(high, upcat[...]) + dot32(rest, upcat[...])
        sent[k] = total.astype(jnp.bfloat16)
        for o in range(1, devices):
            part_copy(k, o).start()
        got[0, pl.ds(pl.multiple_of(source * slots, slots), slots), :] = sent[
            k, pl.ds(pl.multiple_of(me * slots, slots), slots), :
        ]
        return carry

    lax.fori_loop(0, devices, step, 0)

    mine = (token_owner[...] == me.astype(jnp.float32)).astype(jnp.float32)
    fresh = devices * slots
    prior = (iota((fresh, devices), 1) < iota((fresh, devices), 0) // slots).astype(jnp.float32)
    past = jnp.sum(
        dot32(prior.astype(jnp.bfloat16), mine.astype(jnp.bfloat16)), axis=1, keepdims=True
    )
    context = jnp.sum(
        jnp.where(iota((1, devices), 1) == me, context_ref[...].astype(jnp.float32), 0.0),
        axis=1,
        keepdims=True,
    )
    position = context + past + (iota((fresh, 1), 0) % slots).astype(jnp.float32)
    count = jnp.sum(mine, axis=1, keepdims=True)
    fresh_count = jnp.sum(
        jnp.where(iota((devices, fresh), 1) // slots == iota((devices, fresh), 0), count, 0.0),
        axis=0,
        keepdims=True,
    )
    fresh_valid = (iota((1, fresh), 1) % slots).astype(jnp.float32) < fresh_count
    half_size = HEAD // 2
    lane = iota((1, HEAD), 1)
    exponent = (lane % half_size).astype(jnp.float32) * (2.0 / HEAD)
    frequency = jnp.exp(-jnp.log(jnp.full((1, HEAD), rope_base, jnp.float32)) * exponent)
    angle = position * frequency
    cosine = jnp.cos(angle)
    sine = jnp.sin(angle)
    sine = jnp.where(lane < half_size, -sine, sine)

    for copy in locals_[4:]:
        copy.wait()
    kv_local = width // HEAD
    members = HEADS // KV_HEADS
    scale = HEAD ** (-0.5)
    query = query_ref[...].astype(jnp.float32)
    old_count = oldk.shape[0]
    old_valid = iota((1, old_count), 1).astype(jnp.float32) < context
    queries, old_scores, last_scores = [], [], []
    for h in range(kv_local):
        heads = jnp.concatenate(
            [query[:, (h * members + g) * HEAD : (h * members + g + 1) * HEAD] for g in range(members)],
            axis=0,
        )
        cols = slice(h * HEAD, (h + 1) * HEAD)
        queries.append(heads.astype(jnp.bfloat16))
        old_scores.append(
            jnp.where(old_valid, dot_rows(queries[h], oldk[:, cols]) * scale, -1e30)
        )
        last_scores.append(
            jnp.sum(heads * lastk_ref[:, cols].astype(jnp.float32), axis=1, keepdims=True) * scale
        )

    def settle(k, carry):
        for o in range(1, devices):
            part_copy(k, o).wait_recv()
        return carry

    lax.fori_loop(0, devices, settle, 0)
    for h in range(kv_local):
        cols = slice(h * HEAD, (h + 1) * HEAD)
        key = got[0, :, cols].astype(jnp.float32)
        value = got[0, :, width + h * HEAD : width + (h + 1) * HEAD].astype(jnp.float32)
        for o in range(1, devices):
            key = key + got[o, :, cols].astype(jnp.float32)
            value = value + got[o, :, width + h * HEAD : width + (h + 1) * HEAD].astype(jnp.float32)
        key = (key * cosine + pltpu.roll(key, half_size, 1) * sine).astype(jnp.bfloat16)
        value = value.astype(jnp.bfloat16)
        fresh_scores = jnp.where(fresh_valid, dot_rows(queries[h], key) * scale, -1e30)
        top = jnp.maximum(
            jnp.maximum(
                jnp.max(old_scores[h], axis=1, keepdims=True),
                jnp.max(fresh_scores, axis=1, keepdims=True),
            ),
            last_scores[h],
        )
        old_weights = jnp.exp(old_scores[h] - top)
        fresh_weights = jnp.exp(fresh_scores - top)
        last_weight = jnp.exp(last_scores[h] - top)
        total = (
            jnp.sum(old_weights, axis=1, keepdims=True)
            + jnp.sum(fresh_weights, axis=1, keepdims=True)
            + last_weight
        )
        mixed = dot32((old_weights / total).astype(jnp.bfloat16), oldv[:, cols])
        mixed = mixed + dot32((fresh_weights / total).astype(jnp.bfloat16), value)
        mixed = mixed + (last_weight / total).astype(jnp.bfloat16).astype(jnp.float32) * lastv_ref[
            :, cols
        ].astype(jnp.float32)
        mixes[me, pl.ds(h * members, members), :] = mixed.astype(jnp.bfloat16).astype(jnp.float32)

    def mix_copy(o, row):
        return pltpu.make_async_remote_copy(
            src_ref=mixes.at[row],
            dst_ref=mixes.at[row],
            send_sem=ms_sem.at[o],
            recv_sem=mr_sem.at[o],
            device_id=(group, ahead(o), core),
            device_id_type=pl.DeviceIdType.MESH,
        )

    for o in range(1, devices):
        mix_copy(o, me).start()
    for o in range(1, devices):
        mix_copy(o, behind(o)).wait_recv()
    everyone = jnp.concatenate(
        [mixes[:, h, :] for h in range(kv_local * members)], axis=1
    ).astype(jnp.bfloat16)
    narrowed = dot32(everyone, ado[...])
    row_of = jnp.sum(
        jnp.where(iota((devices, devices), 0) == iota((devices, devices), 1), adapters, 0.0),
        axis=1,
        keepdims=True,
    )
    narrow_adapter = (
        (iota((devices, narrowed.shape[1]), 1) % (ADAPTER_COUNT * LOW_RANK)) // LOW_RANK
    ).astype(jnp.float32)
    high, rest = halves(jnp.where(narrow_adapter == row_of, narrowed, 0.0))
    part[...] = dot32(everyone, wo[...]) + dot32(high, auo[...]) + dot32(rest, auo[...])
    swap = pltpu.make_async_remote_copy(
        src_ref=part,
        dst_ref=other,
        send_sem=ts_sem,
        recv_sem=tr_sem,
        device_id=partner,
        device_id_type=pl.DeviceIdType.MESH,
    )
    swap.start()

    for k in range(1, devices):
        x_copy(k).wait_send()
        forward(k).wait_send()
        mix_copy(k, me).wait_send()

    def drain(k, carry):
        for o in range(1, devices):
            part_copy(k, o).wait_send()
        return carry

    lax.fori_loop(0, devices, drain, 0)
    swap.wait()
    out_ref[...] = (part[...] + other[...]).astype(jnp.bfloat16)


def fused(
    side,
    prompt_activations,
    key_matrix,
    value_matrix,
    adapter_down_keyvalue,
    adapter_up_key,
    adapter_up_value,
    request_adapter,
    page_request,
    context_tokens,
    step_query,
    step_key,
    step_value,
    stored_keys,
    stored_values,
    output_matrix,
    adapter_down_output,
    adapter_up_output,
):
    devices = lax.axis_size("dev")
    tok, _ = prompt_activations.shape
    depth, width = key_matrix.shape
    low = adapter_down_keyvalue.shape[1]
    capacity = slots_of(tok // PAGE, devices)
    slots = capacity * PAGE
    rows = request_adapter.shape[0]
    heads = step_query.shape[1] // HEAD
    out_width = output_matrix.shape[1]
    bf16, f32 = jnp.bfloat16, jnp.float32
    whole = pl.BlockSpec(memory_space=pltpu.VMEM)
    far = pl.BlockSpec(memory_space=pl.ANY)
    dma = pltpu.SemaphoreType.DMA
    return pl.pallas_call(
        functools.partial(fused_kernel, devices, side, capacity),
        out_shape=jax.ShapeDtypeStruct((rows, out_width), bf16),
        in_specs=[far] * 4 + [whole] * 8 + [far] * 5,
        out_specs=whole,
        scratch_shapes=[
            pltpu.VMEM((devices, tok, depth), bf16),
            pltpu.VMEM((depth, 2 * width + low), bf16),
            pltpu.VMEM((low, 2 * width), bf16),
            pltpu.VMEM((devices, tok), f32),
            pltpu.VMEM((devices, devices * slots, 2 * width), bf16),
            pltpu.VMEM((devices, devices * slots, 2 * width), bf16),
            pltpu.VMEM(stored_keys.shape[1:], bf16),
            pltpu.VMEM(stored_values.shape[1:], bf16),
            pltpu.VMEM(output_matrix.shape, bf16),
            pltpu.VMEM(adapter_down_output.shape, bf16),
            pltpu.VMEM(adapter_up_output.shape, bf16),
            pltpu.VMEM((devices, heads, HEAD), f32),
            pltpu.VMEM((rows, out_width), f32),
            pltpu.VMEM((rows, out_width), f32),
            dma((9,)),
            dma((devices,)),
            dma((devices,)),
            dma((devices,)),
            dma((devices,)),
            dma((devices, devices)),
            dma((devices, devices)),
            dma((devices,)),
            dma((devices,)),
            dma,
            dma,
        ],
        compiler_params=pltpu.CompilerParams(
            collective_id=0, has_side_effects=True, vmem_limit_bytes=60 * 1024 * 1024
        ),
    )(
        prompt_activations,
        key_matrix,
        value_matrix,
        adapter_down_keyvalue,
        adapter_up_key,
        adapter_up_value,
        request_adapter.reshape(1, -1),
        page_request.reshape(devices, -1),
        context_tokens.reshape(1, -1),
        step_query,
        step_key,
        step_value,
        stored_keys[0],
        stored_values[0],
        output_matrix,
        adapter_down_output,
        adapter_up_output,
    )


def slots_of(pages_here, devices):
    return max(2, (pages_here + devices - 1) // devices)


def choose(*args):
    devices = lax.axis_size("dev")
    tok = args[0].shape[0]
    depth, width = args[1].shape
    slots = slots_of(tok // PAGE, devices) * PAGE
    fits = (
        lax.axis_size("tp") == 2
        and args[6].shape[0] == devices
        and devices % 2 == 0
        and devices <= 16
        and devices * slots == tok
        and tok <= 256
        and depth % 128 == 0
        and width % HEAD == 0
        and slots % 16 == 0
    )
    if fits:
        return fused(2, *args)
    return per_device(*args)


def solution(mesh):
    return jax.shard_map(
        choose,
        mesh=mesh,
        in_specs=(
            P(("group", "dev"), None),
            P("dev", "tp"),
            P("dev", "tp"),
            P("dev", None),
            P(None, "tp"),
            P(None, "tp"),
            P("group"),
            P("group", None),
            P("group"),
            P(("group", "dev"), "tp"),
            P(("group", "dev"), "tp"),
            P(("group", "dev"), "tp"),
            P(("group", "dev"), None, "tp"),
            P(("group", "dev"), None, "tp"),
            P("tp", "dev"),
            P("tp", None),
            P(None, "dev"),
        ),
        out_specs=P("group", "dev"),
        check_vma=False,
    )
```

```python
import functools

import jax
import jax.numpy as jnp
from jax import lax
from jax.experimental import pallas as pl
from jax.experimental.pallas import tpu as pltpu
from jax.sharding import PartitionSpec as P

HEADS = 32
KV_HEADS = 4
HEAD = 128
LOW_RANK = 16
ADAPTER_COUNT = 4
PAGE = 4


adapter_scale = 1.0
rope_base = 500000.0


def rotate(key_rows, positions):
    row_count = key_rows.shape[0]
    blocks = key_rows.reshape(row_count, -1, HEAD)
    half_size = HEAD // 2
    exponent = jnp.arange(half_size, dtype=jnp.float32) * (2.0 / HEAD)
    frequency = jnp.exp(-jnp.log(jnp.float32(rope_base)) * exponent)
    angles = positions.astype(jnp.float32)[:, None] * frequency[None, :]
    cosine = jnp.cos(angles)[:, None, :]
    sine_part = jnp.sin(angles)[:, None, :]
    first_half = blocks[..., :half_size]
    second_half = blocks[..., half_size:]
    turned = jnp.concatenate(
        [
            first_half * cosine - second_half * sine_part,
            second_half * cosine + first_half * sine_part,
        ],
        axis=-1,
    )
    return turned.reshape(row_count, -1)


def owner_ranks(owners, row_total):
    onehot = (owners[:, None] == jnp.arange(row_total, dtype=jnp.int32)[None, :]).astype(jnp.int32)
    before = jnp.cumsum(onehot, axis=0) - onehot
    rank = jnp.sum(before * onehot, axis=1)
    return (onehot, rank)


def mask_columns(narrowed, adapter_list):
    column = jnp.arange(narrowed.shape[1], dtype=jnp.int32)
    owner = column % (ADAPTER_COUNT * LOW_RANK) // LOW_RANK
    return jnp.where(owner[None, :] == adapter_list[:, None], narrowed, jnp.zeros_like(narrowed))


def selected_narrow(activation_rows, adapter_down, adapter_list):
    narrowed = jnp.dot(activation_rows, adapter_down, preferred_element_type=jnp.float32)
    return mask_columns(narrowed, adapter_list)


def widened(selected_rows, up_key, up_value):
    split_at = ADAPTER_COUNT * LOW_RANK
    highest = lax.Precision.HIGHEST
    key_portion = jnp.dot(
        selected_rows[:, :split_at], up_key.astype(jnp.float32), precision=highest
    )
    value_portion = jnp.dot(
        selected_rows[:, split_at:], up_value.astype(jnp.float32), precision=highest
    )
    return (adapter_scale * key_portion, adapter_scale * value_portion)


def attend_local(
    query,
    old_keys,
    old_values,
    old_length,
    fresh_keys,
    fresh_values,
    fresh_valid,
    last_key,
    last_value,
):
    group_size = HEADS // KV_HEADS
    query_heads = query.reshape(-1, group_size, HEAD)
    kv_local = query_heads.shape[0]
    scale_factor = HEAD ** (-0.5)

    def score_of(key_rows):
        shaped = key_rows.reshape(key_rows.shape[0], kv_local, HEAD)
        return (
            jnp.einsum("kgd,lkd->kgl", query_heads, shaped, preferred_element_type=jnp.float32)
            * scale_factor
        )

    def mix_with(probs, value_rows):
        shaped = value_rows.reshape(value_rows.shape[0], kv_local, HEAD)
        return jnp.einsum("kgl,lkd->kgd", probs, shaped, preferred_element_type=jnp.float32)

    old_valid = jnp.arange(old_keys.shape[0], dtype=jnp.int32) < old_length
    old_scores = jnp.where(old_valid[None, None, :], score_of(old_keys), -1e30)
    fresh_scores = jnp.where(fresh_valid[None, None, :], score_of(fresh_keys), -1e30)
    last_score = score_of(last_key[None, :])
    top = jnp.maximum(
        jnp.maximum(
            jnp.max(old_scores, axis=-1, keepdims=True),
            jnp.max(fresh_scores, axis=-1, keepdims=True),
        ),
        last_score,
    )
    old_weights = jnp.exp(old_scores - top)
    fresh_weights = jnp.exp(fresh_scores - top)
    last_weight = jnp.exp(last_score - top)
    total = (
        jnp.sum(old_weights, axis=-1, keepdims=True)
        + jnp.sum(fresh_weights, axis=-1, keepdims=True)
        + last_weight
    )
    output = mix_with((old_weights / total).astype(jnp.bfloat16), old_values)
    output = output + mix_with((fresh_weights / total).astype(jnp.bfloat16), fresh_values)
    output = output + mix_with((last_weight / total).astype(jnp.bfloat16), last_value[None, :])
    return output.reshape(-1).astype(jnp.bfloat16)


def per_device(
    prompt_activations,
    key_matrix,
    value_matrix,
    adapter_down_keyvalue,
    adapter_up_key,
    adapter_up_value,
    request_adapter,
    page_request,
    context_tokens,
    step_query,
    step_key,
    step_value,
    stored_keys,
    stored_values,
    output_matrix,
    adapter_down_output,
    adapter_up_output,
):
    devices = lax.axis_size("dev")
    device = lax.axis_index("dev")
    tok_count = prompt_activations.shape[0]
    pages_here = tok_count // PAGE
    capacity = max(2, (pages_here + devices - 1) // devices)
    row_total = request_adapter.shape[0]
    owners = page_request[:, 0]
    onehot, rank = owner_ranks(owners, row_total)
    first_page = device * pages_here
    my_owners = lax.dynamic_slice_in_dim(owners, first_page, pages_here, 0)
    my_rank = lax.dynamic_slice_in_dim(rank, first_page, pages_here, 0)
    tokens = jnp.arange(tok_count, dtype=jnp.int32)
    token_page = tokens // PAGE
    token_owner = jnp.take(my_owners, token_page)
    position = (
        jnp.take(context_tokens, token_owner) + jnp.take(my_rank, token_page) * PAGE + tokens % PAGE
    )
    adapter_list = jnp.take(request_adapter, token_owner)
    key_width = key_matrix.shape[1]

    def add_rows(portion):
        return jnp.dot(prompt_activations, portion, preferred_element_type=jnp.float32)

    key_raw = add_rows(lax.all_gather(key_matrix, "dev", axis=0, tiled=True))
    value_raw = add_rows(lax.all_gather(value_matrix, "dev", axis=0, tiled=True))
    down_complete = lax.all_gather(adapter_down_keyvalue, "dev", axis=0, tiled=True)
    narrowed = jnp.dot(prompt_activations, down_complete, preferred_element_type=jnp.float32)
    selected_rows = mask_columns(narrowed, adapter_list)
    key_delta, value_delta = widened(selected_rows, adapter_up_key, adapter_up_value)
    key_rows = rotate(key_raw + key_delta, position).astype(jnp.bfloat16)
    value_rows = (value_raw + value_delta).astype(jnp.bfloat16)
    joined_rows = jnp.concatenate([key_rows, value_rows], axis=1)
    local_hot = (my_owners[:, None] == jnp.arange(row_total, dtype=jnp.int32)[None, :]).astype(
        jnp.int32
    )
    local_before = jnp.cumsum(local_hot, axis=0) - local_hot
    local_slot = jnp.sum(local_before * local_hot, axis=1)
    peer_slots = capacity * PAGE
    target = token_owner * peer_slots + jnp.take(local_slot, token_page) * PAGE + tokens % PAGE
    outgoing = (
        jnp.zeros((devices * peer_slots, 2 * key_width), jnp.bfloat16).at[target].set(joined_rows)
    )
    outgoing = outgoing.reshape(devices, peer_slots, 2 * key_width)
    incoming = lax.all_to_all(outgoing, "dev", split_axis=0, concat_axis=0, tiled=True)
    fresh_keys = incoming[:, :, :key_width].reshape(-1, key_width)
    fresh_values = incoming[:, :, key_width:].reshape(-1, key_width)
    my_column = jnp.take(onehot, device, axis=1)
    count_from = jnp.sum(my_column.reshape(devices, pages_here), axis=1)
    slot_page = jnp.arange(peer_slots, dtype=jnp.int32) // PAGE
    fresh_valid = (slot_page[None, :] < count_from[:, None]).reshape(-1)
    mixed_local = attend_local(
        step_query[0],
        stored_keys[0],
        stored_values[0],
        jnp.take(context_tokens, device),
        fresh_keys,
        fresh_values,
        fresh_valid,
        step_key[0],
        step_value[0],
    ).reshape(1, -1)
    portion = lax.all_gather(mixed_local, "dev", axis=0, tiled=True)
    plain_result = jnp.dot(portion, output_matrix, preferred_element_type=jnp.float32)
    selected_output = selected_narrow(portion, adapter_down_output, request_adapter)
    partial_output = plain_result + adapter_scale * jnp.dot(
        selected_output, adapter_up_output.astype(jnp.float32), precision=lax.Precision.HIGHEST
    )
    return lax.psum(partial_output, "tp").astype(jnp.bfloat16)


def iota(shape, axis):
    return lax.broadcasted_iota(jnp.int32, shape, axis)


def dot32(a, b):
    return jnp.dot(a, b, preferred_element_type=jnp.float32)


def dot_rows(a, b):
    return lax.dot_general(a, b, (((1,), (1,)), ((), ())), preferred_element_type=jnp.float32)


def halves(value):
    high = value.astype(jnp.bfloat16)
    return high, (value - high.astype(jnp.float32)).astype(jnp.bfloat16)


def fused_kernel(
    devices,
    side,
    capacity,
    x_hbm,
    wk_hbm,
    wv_hbm,
    ad_hbm,
    upk_ref,
    upv_ref,
    adapter_ref,
    owner_ref,
    context_ref,
    query_ref,
    lastk_ref,
    lastv_ref,
    oldk_hbm,
    oldv_hbm,
    wo_hbm,
    ado_hbm,
    auo_hbm,
    out_ref,
    raw,
    acts,
    weights,
    upcat,
    token_owner,
    shipped,
    landed,
    sent,
    got,
    oldk,
    oldv,
    wo,
    ado,
    auo,
    mixes,
    part,
    other,
    local_sem,
    xs_sem,
    xr_sem,
    fs_sem,
    fr_sem,
    zs_sem,
    zr_sem,
    ys_sem,
    yr_sem,
    qs_sem,
    qr_sem,
    es_sem,
    er_sem,
    ps_sem,
    pr_sem,
    ms_sem,
    mr_sem,
    ts_sem,
    tr_sem,
):
    group = lax.axis_index("group")
    me = lax.axis_index("dev")
    core = lax.axis_index("tp")
    partner = (group, me, 1 - core)
    tok = x_hbm.shape[0]
    depth = wk_hbm.shape[0]
    width = wk_hbm.shape[1]
    low = ad_hbm.shape[1]
    half = tok // 2
    slots = capacity * PAGE
    outer = devices // side
    mz, mx = me // side, me % side
    beside = (group, mz * side + 1 - mx, core)
    across = (1 - group, me, core)
    kv_local = width // HEAD
    chunks = 1 + 2 * kv_local
    mesh_ids = pl.DeviceIdType.MESH

    def ahead(k):
        return ((mz + k // side) % outer) * side + (mx + k % side) % side

    def behind(k):
        return ((mz + outer - k // side) % outer) * side + (mx + side - k % side) % side

    def source_of(j):
        if j == 0:
            return ad_hbm, 0
        if j <= kv_local:
            return wk_hbm, (j - 1) * HEAD
        return wv_hbm, (j - 1 - kv_local) * HEAD

    def rows_of(j, cut):
        if j == 0:
            size = depth // 4
            return pl.ds(pl.multiple_of((cut * 2 + core) * size, size), size)
        size = depth // 2
        return pl.ds(pl.multiple_of(cut * size, size), size)

    def remote(src, dst, send, recv, device):
        return pltpu.make_async_remote_copy(
            src_ref=src,
            dst_ref=dst,
            send_sem=send,
            recv_sem=recv,
            device_id=device,
            device_id_type=mesh_ids,
        )

    own_half = pl.ds(pl.multiple_of(core * half, half), half)

    def columns(b, x):
        return pl.ds(pl.multiple_of((b * side + x) * depth, depth), depth)

    locals_ = []
    for j in range(chunks):
        ref, at = source_of(j)
        locals_.append(
            pltpu.make_async_copy(ref.at[:, pl.ds(at, HEAD)], weights.at[j, mz], local_sem.at[j])
        )
    for b in range(outer):
        locals_.append(
            pltpu.make_async_copy(
                x_hbm.at[:, columns(b, mx)], raw.at[0, b], local_sem.at[chunks + b]
            )
        )
    rest_at = chunks + outer
    later = [(oldk_hbm, oldk), (oldv_hbm, oldv), (wo_hbm, wo), (ado_hbm, ado), (auo_hbm, auo)]
    for i, (ref, to) in enumerate(later):
        locals_.append(pltpu.make_async_copy(ref, to, local_sem.at[rest_at + i]))

    barrier = pltpu.get_barrier_semaphore()
    for k in range(1, devices):
        pl.semaphore_signal(
            barrier, inc=1, device_id=(group, ahead(k), core), device_id_type=mesh_ids
        )
    pl.semaphore_signal(barrier, inc=1, device_id=partner, device_id_type=mesh_ids)
    pl.semaphore_signal(barrier, inc=1, device_id=across, device_id_type=mesh_ids)
    pl.semaphore_wait(barrier, devices + 1)

    def x_copy(b):
        return remote(
            x_hbm.at[own_half, columns(b, 1 - mx)],
            raw.at[1, b, own_half],
            xs_sem.at[b],
            xr_sem.at[b],
            beside,
        )

    def x_forward(b):
        view = raw.at[1, b, own_half]
        return remote(view, view, fs_sem.at[b], fr_sem.at[b], partner)

    def z_first(j, up):
        ref, at = source_of(j)
        to = mz + 1 if up else mz - 1
        return remote(
            ref.at[rows_of(j, group), pl.ds(at, HEAD)],
            weights.at[j, mz, rows_of(j, group)],
            zs_sem.at[j, mz, 0 if up else 1],
            zr_sem.at[j, mz],
            (group, to * side + mx, core),
        )

    def z_relay(j, b, up):
        view = weights.at[j, b, rows_of(j, group)]
        to = mz + 1 if up else mz - 1
        return remote(
            view,
            view,
            zs_sem.at[j, b, 0 if up else 1],
            zr_sem.at[j, b],
            (group, to * side + mx, core),
        )

    def y_copy(j, b):
        view = weights.at[j, b, rows_of(j, group)]
        return remote(view, view, ys_sem.at[j, b], yr_sem.at[j, b], across)

    def y_arrival(j, b):
        view = weights.at[j, b, rows_of(j, 1 - group)]
        return remote(view, view, ys_sem.at[j, b], yr_sem.at[j, b], across)

    def q_copy(b, cut, which):
        view = weights.at[0, b, rows_of(0, cut)]
        return remote(view, view, qs_sem.at[b, which], qr_sem.at[b, which], partner)

    def issue(j):
        @pl.when(mz < outer - 1)
        def _():
            z_first(j, True).start()

        @pl.when(mz > 0)
        def _():
            z_first(j, False).start()

    def relay(j):
        for t in range(1, outer):
            for up in (True, False):
                b = mz - t if up else mz + t

                @pl.when(b >= 0 if up else b < outer)
                def _():
                    z_relay(j, b, up).wait_recv()

                    @pl.when(mz < outer - 1 if up else mz > 0)
                    def _():
                        z_relay(j, b, up).start()

                    y_copy(j, b).start()
                    if j == 0:
                        q_copy(b, group, 0).start()

    def others(body):
        for t in range(1, outer):
            body((mz + t) % outer)

    def gather(j):
        if j == 0:

            def pass_on(b):
                y_arrival(0, b).wait_recv()
                q_copy(b, 1 - group, 1).start()

            def take(b):
                q_copy(b, group, 0).wait_recv()
                q_copy(b, 1 - group, 1).wait_recv()

            others(pass_on)
            others(take)
        else:
            others(lambda b: y_arrival(j, b).wait_recv())

    def part_copy(j, o):
        peer = ahead(o)
        return remote(
            sent.at[j, pl.ds(pl.multiple_of(peer * slots, slots), slots)],
            got.at[j, pl.ds(pl.multiple_of(me * slots, slots), slots)],
            ps_sem.at[j, o],
            pr_sem.at[j, o],
            (group, peer, core),
        )

    def part_arrival(j, o):
        peer = behind(o)
        return remote(
            sent.at[j, pl.ds(pl.multiple_of(peer * slots, slots), slots)],
            got.at[j, pl.ds(pl.multiple_of(peer * slots, slots), slots)],
            ps_sem.at[j, o],
            pr_sem.at[j, o],
            (group, peer, core),
        )

    def exchange(j):
        return remote(shipped.at[j], landed.at[j], es_sem.at[j], er_sem.at[j], beside)

    issue(0)
    issue(1)
    for b in range(outer):
        x_copy(b).start()
    for copy in locals_:
        copy.start()

    pages = owner_ref.shape[1]
    spread = (iota((pages, tok), 1) // PAGE == iota((pages, tok), 0)).astype(jnp.bfloat16)
    token_owner[...] = dot32(owner_ref[...].astype(jnp.float32).astype(jnp.bfloat16), spread)
    earlier = (iota((tok, tok), 0) // PAGE < iota((tok, tok), 1) // PAGE).astype(jnp.bfloat16)
    lora = low // 2
    fresh = devices * slots
    upcat[...] = jnp.zeros_like(upcat)
    upcat[pl.ds(0, lora), pl.ds(0, width)] = upk_ref[...]
    upcat[pl.ds(lora, lora), pl.ds(width, width)] = upv_ref[...]
    adapters = adapter_ref[...].astype(jnp.float32)
    slot_rows = devices * slots
    row_adapter = jnp.sum(
        jnp.where(iota((slot_rows, devices), 0) // slots == iota((slot_rows, devices), 1), adapters, 0.0),
        axis=1,
        keepdims=True,
    )
    low_adapter = ((iota((slot_rows, low), 1) % lora) // LOW_RANK).astype(jnp.float32)
    keep_low = low_adapter == row_adapter

    def mover(source):
        owners = token_owner[pl.ds(source, 1), :]
        hot = (iota((devices, tok), 0).astype(jnp.float32) == owners).astype(jnp.float32)
        before = dot32(hot.astype(jnp.bfloat16), earlier)
        rank = jnp.sum(before * hot, axis=0, keepdims=True)
        place = owners * float(slots) + rank + (iota((1, tok), 1) % PAGE).astype(jnp.float32)
        return (iota((fresh, tok), 0).astype(jnp.float32) == place).astype(jnp.bfloat16)

    row_owner = (iota((fresh, 1), 0) // slots).astype(jnp.float32)
    contexts = context_ref[...].astype(jnp.float32)
    start_at = jnp.sum(
        jnp.where(iota((fresh, devices), 0) // slots == iota((fresh, devices), 1), contexts, 0.0),
        axis=1,
        keepdims=True,
    )
    ahead_of = jnp.zeros((fresh, tok), jnp.float32)
    for block in range(devices):
        line = jnp.where(block < me, token_owner[block : block + 1, :], -1.0)
        ahead_of = ahead_of + (line == row_owner).astype(jnp.float32)
    position = (
        start_at
        + jnp.sum(ahead_of, axis=1, keepdims=True)
        + (iota((fresh, 1), 0) % slots).astype(jnp.float32)
    )
    half_size = HEAD // 2
    lane = iota((1, HEAD), 1)
    exponent = (lane % half_size).astype(jnp.float32) * (2.0 / HEAD)
    frequency = jnp.exp(-jnp.log(jnp.full((1, HEAD), rope_base, jnp.float32)) * exponent)
    angle = position * frequency
    cosine = jnp.cos(angle)
    sine = jnp.sin(angle)
    sine = jnp.where(lane < half_size, -sine, sine)

    relay(0)
    issue(2)
    own_move = mover(me)
    for b in range(outer):
        locals_[chunks + b].wait()
        acts[0, b] = dot32(own_move, raw[0, b]).astype(jnp.bfloat16)
    gather(0)
    relay(1)
    issue(3)
    gather(1)
    relay(2)
    issue(4)
    for b in range(outer):
        x_copy(b).wait_recv()
        x_forward(b).start()
    side_move = mover(mz * side + 1 - mx)
    for b in range(outer):
        x_forward(b).wait_recv()
        acts[1, b] = dot32(side_move, raw[1, b]).astype(jnp.bfloat16)
    for copy in locals_[:chunks]:
        copy.wait()

    def product(i, j):
        total = dot32(acts[i, 0], weights[j, 0])
        for b in range(1, outer):
            total = total + dot32(acts[i, b], weights[j, b])
        return total

    def multiply(j):
        shipped[j] = product(1, j)
        exchange(j).start()
        return product(0, j)

    def finish(j, own, low_parts):
        exchange(j).wait_recv()
        total = own + landed[j]
        at = (j - 1) * HEAD
        for piece in low_parts:
            total = total + dot32(piece, upcat[:, at : at + HEAD])
        if j <= kv_local:
            total = total * cosine + pltpu.roll(total, half_size, 1) * sine
        sent[j] = total.astype(jnp.bfloat16)
        for o in range(1, devices):
            part_copy(j, o).start()
        mine_at = pl.ds(pl.multiple_of(me * slots, slots), slots)
        got[j, mine_at, :] = sent[j, mine_at, :]

    own_low = multiply(0)
    own_1 = multiply(1)
    gather(2)
    own_2 = multiply(2)
    exchange(0).wait_recv()
    low_parts = halves(jnp.where(keep_low, own_low + landed[0], 0.0))
    finish(1, own_1, low_parts)
    relay(3)
    finish(2, own_2, low_parts)
    gather(3)
    own_3 = multiply(3)
    relay(4)
    finish(3, own_3, low_parts)
    gather(4)
    own_4 = multiply(4)

    mine = (token_owner[...] == me.astype(jnp.float32)).astype(jnp.float32)
    context = jnp.sum(
        jnp.where(iota((1, devices), 1) == me, context_ref[...].astype(jnp.float32), 0.0),
        axis=1,
        keepdims=True,
    )
    count = jnp.sum(mine, axis=1, keepdims=True)
    fresh_count = jnp.sum(
        jnp.where(iota((devices, fresh), 1) // slots == iota((devices, fresh), 0), count, 0.0),
        axis=0,
        keepdims=True,
    )
    fresh_valid = (iota((1, fresh), 1) % slots).astype(jnp.float32) < fresh_count
    for copy in locals_[rest_at:]:
        copy.wait()
    members = HEADS // KV_HEADS
    scale = HEAD ** (-0.5)
    query = query_ref[...].astype(jnp.float32)
    old_count = oldk.shape[0]
    old_valid = iota((1, old_count), 1).astype(jnp.float32) < context
    queries, old_scores, last_scores = [], [], []
    for h in range(kv_local):
        heads = jnp.concatenate(
            [query[:, (h * members + g) * HEAD : (h * members + g + 1) * HEAD] for g in range(members)],
            axis=0,
        )
        cols = slice(h * HEAD, (h + 1) * HEAD)
        queries.append(heads.astype(jnp.bfloat16))
        old_scores.append(
            jnp.where(old_valid, dot_rows(queries[h], oldk[:, cols]) * scale, -1e30)
        )
        last_scores.append(
            jnp.sum(heads * lastk_ref[:, cols].astype(jnp.float32), axis=1, keepdims=True) * scale
        )

    def settle(j):
        for o in range(1, devices):
            part_arrival(j, o).wait_recv()

    fresh_scores_of = []
    for h in range(kv_local):
        settle(1 + h)
        fresh_scores_of.append(
            jnp.where(fresh_valid, dot_rows(queries[h], got[1 + h]) * scale, -1e30)
        )
    finish(4, own_4, low_parts)
    for h in range(kv_local):
        cols = slice(h * HEAD, (h + 1) * HEAD)
        fresh_scores = fresh_scores_of[h]
        top = jnp.maximum(
            jnp.maximum(
                jnp.max(old_scores[h], axis=1, keepdims=True),
                jnp.max(fresh_scores, axis=1, keepdims=True),
            ),
            last_scores[h],
        )
        old_weights = jnp.exp(old_scores[h] - top)
        fresh_weights = jnp.exp(fresh_scores - top)
        last_weight = jnp.exp(last_scores[h] - top)
        total = (
            jnp.sum(old_weights, axis=1, keepdims=True)
            + jnp.sum(fresh_weights, axis=1, keepdims=True)
            + last_weight
        )
        settle(1 + kv_local + h)
        value = got[1 + kv_local + h]
        mixed = dot32((old_weights / total).astype(jnp.bfloat16), oldv[:, cols])
        mixed = mixed + dot32((fresh_weights / total).astype(jnp.bfloat16), value)
        mixed = mixed + (last_weight / total).astype(jnp.bfloat16).astype(jnp.float32) * lastv_ref[
            :, cols
        ].astype(jnp.float32)
        mixes[me, pl.ds(h * members, members), :] = mixed.astype(jnp.bfloat16).astype(jnp.float32)

    def mix_copy(o, row):
        return pltpu.make_async_remote_copy(
            src_ref=mixes.at[row],
            dst_ref=mixes.at[row],
            send_sem=ms_sem.at[o],
            recv_sem=mr_sem.at[o],
            device_id=(group, ahead(o), core),
            device_id_type=pl.DeviceIdType.MESH,
        )

    for o in range(1, devices):
        mix_copy(o, me).start()
    for o in range(1, devices):
        mix_copy(o, behind(o)).wait_recv()
    everyone = jnp.concatenate(
        [mixes[:, h, :] for h in range(kv_local * members)], axis=1
    ).astype(jnp.bfloat16)
    narrowed = dot32(everyone, ado[...])
    row_of = jnp.sum(
        jnp.where(iota((devices, devices), 0) == iota((devices, devices), 1), adapters, 0.0),
        axis=1,
        keepdims=True,
    )
    narrow_adapter = (
        (iota((devices, narrowed.shape[1]), 1) % (ADAPTER_COUNT * LOW_RANK)) // LOW_RANK
    ).astype(jnp.float32)
    high, rest = halves(jnp.where(narrow_adapter == row_of, narrowed, 0.0))
    part[...] = dot32(everyone, wo[...]) + dot32(high, auo[...]) + dot32(rest, auo[...])
    swap = pltpu.make_async_remote_copy(
        src_ref=part,
        dst_ref=other,
        send_sem=ts_sem,
        recv_sem=tr_sem,
        device_id=partner,
        device_id_type=pl.DeviceIdType.MESH,
    )
    swap.start()

    for b in range(outer):
        x_copy(b).wait_send()
        x_forward(b).wait_send()
    for o in range(1, devices):
        mix_copy(o, me).wait_send()
    for j in range(chunks):
        exchange(j).wait_send()
        if j > 0:
            for o in range(1, devices):
                part_copy(j, o).wait_send()

        @pl.when(mz < outer - 1)
        def _():
            z_first(j, True).wait_send()

        @pl.when(mz > 0)
        def _():
            z_first(j, False).wait_send()

        for t in range(1, outer):
            for up in (True, False):
                b = mz - t if up else mz + t

                @pl.when(b >= 0 if up else b < outer)
                def _():
                    @pl.when(mz < outer - 1 if up else mz > 0)
                    def _():
                        z_relay(j, b, up).wait_send()

                    y_copy(j, b).wait_send()
                    if j == 0:
                        q_copy(b, group, 0).wait_send()
                        q_copy(b, 1 - group, 1).wait_send()

    swap.wait()
    out_ref[...] = (part[...] + other[...]).astype(jnp.bfloat16)


def fused(
    side,
    prompt_activations,
    key_matrix,
    value_matrix,
    adapter_down_keyvalue,
    adapter_up_key,
    adapter_up_value,
    request_adapter,
    page_request,
    context_tokens,
    step_query,
    step_key,
    step_value,
    stored_keys,
    stored_values,
    output_matrix,
    adapter_down_output,
    adapter_up_output,
):
    devices = lax.axis_size("dev")
    tok, _ = prompt_activations.shape
    depth, width = key_matrix.shape
    low = adapter_down_keyvalue.shape[1]
    capacity = slots_of(tok // PAGE, devices)
    slots = capacity * PAGE
    rows = request_adapter.shape[0]
    heads = step_query.shape[1] // HEAD
    outer = devices // side
    chunks = 1 + 2 * (width // HEAD)
    fresh = devices * slots
    out_width = output_matrix.shape[1]
    bf16, f32 = jnp.bfloat16, jnp.float32
    whole = pl.BlockSpec(memory_space=pltpu.VMEM)
    far = pl.BlockSpec(memory_space=pl.ANY)
    dma = pltpu.SemaphoreType.DMA
    return pl.pallas_call(
        functools.partial(fused_kernel, devices, side, capacity),
        out_shape=jax.ShapeDtypeStruct((rows, out_width), bf16),
        in_specs=[far] * 4 + [whole] * 8 + [far] * 5,
        out_specs=whole,
        scratch_shapes=[
            pltpu.VMEM((2, outer, tok, depth), bf16),
            pltpu.VMEM((2, outer, tok, depth), bf16),
            pltpu.VMEM((chunks, outer, depth, HEAD), bf16),
            pltpu.VMEM((low, 2 * width), bf16),
            pltpu.VMEM((devices, tok), f32),
            pltpu.VMEM((chunks, fresh, HEAD), f32),
            pltpu.VMEM((chunks, fresh, HEAD), f32),
            pltpu.VMEM((chunks, fresh, HEAD), bf16),
            pltpu.VMEM((chunks, fresh, HEAD), bf16),
            pltpu.VMEM(stored_keys.shape[1:], bf16),
            pltpu.VMEM(stored_values.shape[1:], bf16),
            pltpu.VMEM(output_matrix.shape, bf16),
            pltpu.VMEM(adapter_down_output.shape, bf16),
            pltpu.VMEM(adapter_up_output.shape, bf16),
            pltpu.VMEM((devices, heads, HEAD), f32),
            pltpu.VMEM((rows, out_width), f32),
            pltpu.VMEM((rows, out_width), f32),
            dma((chunks + outer + 5,)),
            dma((outer,)),
            dma((outer,)),
            dma((outer,)),
            dma((outer,)),
            dma((chunks, outer, 2)),
            dma((chunks, outer)),
            dma((chunks, outer)),
            dma((chunks, outer)),
            dma((outer, 2)),
            dma((outer, 2)),
            dma((chunks,)),
            dma((chunks,)),
            dma((chunks, devices)),
            dma((chunks, devices)),
            dma((devices,)),
            dma((devices,)),
            dma,
            dma,
        ],
        compiler_params=pltpu.CompilerParams(
            collective_id=0, has_side_effects=True, vmem_limit_bytes=60 * 1024 * 1024
        ),
    )(
        prompt_activations,
        key_matrix,
        value_matrix,
        adapter_down_keyvalue,
        adapter_up_key,
        adapter_up_value,
        request_adapter.reshape(1, -1),
        page_request.reshape(devices, -1),
        context_tokens.reshape(1, -1),
        step_query,
        step_key,
        step_value,
        stored_keys[0],
        stored_values[0],
        output_matrix,
        adapter_down_output,
        adapter_up_output,
    )


def slots_of(pages_here, devices):
    return max(2, (pages_here + devices - 1) // devices)


def choose(*args):
    devices = lax.axis_size("dev")
    tok = args[0].shape[0]
    depth, width = args[1].shape
    slots = slots_of(tok // PAGE, devices) * PAGE
    fits = (
        lax.axis_size("tp") == 2
        and lax.axis_size("group") == 2
        and devices >= 4
        and args[6].shape[0] == devices
        and devices % 2 == 0
        and devices <= 16
        and devices * slots == tok
        and tok <= 256
        and depth % 128 == 0
        and width == 2 * HEAD
        and args[3].shape[1] == HEAD
        and slots % 16 == 0
    )
    if fits:
        return fused(2, *args)
    return per_device(*args)


def solution(mesh):
    return jax.shard_map(
        choose,
        mesh=mesh,
        in_specs=(
            P(("group", "dev"), None),
            P("dev", "tp"),
            P("dev", "tp"),
            P("dev", None),
            P(None, "tp"),
            P(None, "tp"),
            P("group"),
            P("group", None),
            P("group"),
            P(("group", "dev"), "tp"),
            P(("group", "dev"), "tp"),
            P(("group", "dev"), "tp"),
            P(("group", "dev"), None, "tp"),
            P(("group", "dev"), None, "tp"),
            P("tp", "dev"),
            P("tp", None),
            P(None, "dev"),
        ),
        out_specs=P("group", "dev"),
        check_vma=False,
    )
```

```python
import functools

import jax
import jax.numpy as jnp
from jax import lax
from jax.experimental import pallas as pl
from jax.experimental.pallas import tpu as pltpu
from jax.sharding import PartitionSpec as P

HEADS = 32
KV_HEADS = 4
HEAD = 128
LOW_RANK = 16
ADAPTER_COUNT = 4
PAGE = 4


adapter_scale = 1.0
rope_base = 500000.0


def rotate(key_rows, positions):
    row_count = key_rows.shape[0]
    blocks = key_rows.reshape(row_count, -1, HEAD)
    half_size = HEAD // 2
    exponent = jnp.arange(half_size, dtype=jnp.float32) * (2.0 / HEAD)
    frequency = jnp.exp(-jnp.log(jnp.float32(rope_base)) * exponent)
    angles = positions.astype(jnp.float32)[:, None] * frequency[None, :]
    cosine = jnp.cos(angles)[:, None, :]
    sine_part = jnp.sin(angles)[:, None, :]
    first_half = blocks[..., :half_size]
    second_half = blocks[..., half_size:]
    turned = jnp.concatenate(
        [
            first_half * cosine - second_half * sine_part,
            second_half * cosine + first_half * sine_part,
        ],
        axis=-1,
    )
    return turned.reshape(row_count, -1)


def owner_ranks(owners, row_total):
    onehot = (owners[:, None] == jnp.arange(row_total, dtype=jnp.int32)[None, :]).astype(jnp.int32)
    before = jnp.cumsum(onehot, axis=0) - onehot
    rank = jnp.sum(before * onehot, axis=1)
    return (onehot, rank)


def mask_columns(narrowed, adapter_list):
    column = jnp.arange(narrowed.shape[1], dtype=jnp.int32)
    owner = column % (ADAPTER_COUNT * LOW_RANK) // LOW_RANK
    return jnp.where(owner[None, :] == adapter_list[:, None], narrowed, jnp.zeros_like(narrowed))


def selected_narrow(activation_rows, adapter_down, adapter_list):
    narrowed = jnp.dot(activation_rows, adapter_down, preferred_element_type=jnp.float32)
    return mask_columns(narrowed, adapter_list)


def widened(selected_rows, up_key, up_value):
    split_at = ADAPTER_COUNT * LOW_RANK
    highest = lax.Precision.HIGHEST
    key_portion = jnp.dot(
        selected_rows[:, :split_at], up_key.astype(jnp.float32), precision=highest
    )
    value_portion = jnp.dot(
        selected_rows[:, split_at:], up_value.astype(jnp.float32), precision=highest
    )
    return (adapter_scale * key_portion, adapter_scale * value_portion)


def attend_local(
    query,
    old_keys,
    old_values,
    old_length,
    fresh_keys,
    fresh_values,
    fresh_valid,
    last_key,
    last_value,
):
    group_size = HEADS // KV_HEADS
    query_heads = query.reshape(-1, group_size, HEAD)
    kv_local = query_heads.shape[0]
    scale_factor = HEAD ** (-0.5)

    def score_of(key_rows):
        shaped = key_rows.reshape(key_rows.shape[0], kv_local, HEAD)
        return (
            jnp.einsum("kgd,lkd->kgl", query_heads, shaped, preferred_element_type=jnp.float32)
            * scale_factor
        )

    def mix_with(probs, value_rows):
        shaped = value_rows.reshape(value_rows.shape[0], kv_local, HEAD)
        return jnp.einsum("kgl,lkd->kgd", probs, shaped, preferred_element_type=jnp.float32)

    old_valid = jnp.arange(old_keys.shape[0], dtype=jnp.int32) < old_length
    old_scores = jnp.where(old_valid[None, None, :], score_of(old_keys), -1e30)
    fresh_scores = jnp.where(fresh_valid[None, None, :], score_of(fresh_keys), -1e30)
    last_score = score_of(last_key[None, :])
    top = jnp.maximum(
        jnp.maximum(
            jnp.max(old_scores, axis=-1, keepdims=True),
            jnp.max(fresh_scores, axis=-1, keepdims=True),
        ),
        last_score,
    )
    old_weights = jnp.exp(old_scores - top)
    fresh_weights = jnp.exp(fresh_scores - top)
    last_weight = jnp.exp(last_score - top)
    total = (
        jnp.sum(old_weights, axis=-1, keepdims=True)
        + jnp.sum(fresh_weights, axis=-1, keepdims=True)
        + last_weight
    )
    output = mix_with((old_weights / total).astype(jnp.bfloat16), old_values)
    output = output + mix_with((fresh_weights / total).astype(jnp.bfloat16), fresh_values)
    output = output + mix_with((last_weight / total).astype(jnp.bfloat16), last_value[None, :])
    return output.reshape(-1).astype(jnp.bfloat16)


def per_device(
    prompt_activations,
    key_matrix,
    value_matrix,
    adapter_down_keyvalue,
    adapter_up_key,
    adapter_up_value,
    request_adapter,
    page_request,
    context_tokens,
    step_query,
    step_key,
    step_value,
    stored_keys,
    stored_values,
    output_matrix,
    adapter_down_output,
    adapter_up_output,
):
    devices = lax.axis_size("dev")
    device = lax.axis_index("dev")
    tok_count = prompt_activations.shape[0]
    pages_here = tok_count // PAGE
    capacity = max(2, (pages_here + devices - 1) // devices)
    row_total = request_adapter.shape[0]
    owners = page_request[:, 0]
    onehot, rank = owner_ranks(owners, row_total)
    first_page = device * pages_here
    my_owners = lax.dynamic_slice_in_dim(owners, first_page, pages_here, 0)
    my_rank = lax.dynamic_slice_in_dim(rank, first_page, pages_here, 0)
    tokens = jnp.arange(tok_count, dtype=jnp.int32)
    token_page = tokens // PAGE
    token_owner = jnp.take(my_owners, token_page)
    position = (
        jnp.take(context_tokens, token_owner) + jnp.take(my_rank, token_page) * PAGE + tokens % PAGE
    )
    adapter_list = jnp.take(request_adapter, token_owner)
    key_width = key_matrix.shape[1]

    def add_rows(portion):
        return jnp.dot(prompt_activations, portion, preferred_element_type=jnp.float32)

    key_raw = add_rows(lax.all_gather(key_matrix, "dev", axis=0, tiled=True))
    value_raw = add_rows(lax.all_gather(value_matrix, "dev", axis=0, tiled=True))
    down_complete = lax.all_gather(adapter_down_keyvalue, "dev", axis=0, tiled=True)
    narrowed = jnp.dot(prompt_activations, down_complete, preferred_element_type=jnp.float32)
    selected_rows = mask_columns(narrowed, adapter_list)
    key_delta, value_delta = widened(selected_rows, adapter_up_key, adapter_up_value)
    key_rows = rotate(key_raw + key_delta, position).astype(jnp.bfloat16)
    value_rows = (value_raw + value_delta).astype(jnp.bfloat16)
    joined_rows = jnp.concatenate([key_rows, value_rows], axis=1)
    local_hot = (my_owners[:, None] == jnp.arange(row_total, dtype=jnp.int32)[None, :]).astype(
        jnp.int32
    )
    local_before = jnp.cumsum(local_hot, axis=0) - local_hot
    local_slot = jnp.sum(local_before * local_hot, axis=1)
    peer_slots = capacity * PAGE
    target = token_owner * peer_slots + jnp.take(local_slot, token_page) * PAGE + tokens % PAGE
    outgoing = (
        jnp.zeros((devices * peer_slots, 2 * key_width), jnp.bfloat16).at[target].set(joined_rows)
    )
    outgoing = outgoing.reshape(devices, peer_slots, 2 * key_width)
    incoming = lax.all_to_all(outgoing, "dev", split_axis=0, concat_axis=0, tiled=True)
    fresh_keys = incoming[:, :, :key_width].reshape(-1, key_width)
    fresh_values = incoming[:, :, key_width:].reshape(-1, key_width)
    my_column = jnp.take(onehot, device, axis=1)
    count_from = jnp.sum(my_column.reshape(devices, pages_here), axis=1)
    slot_page = jnp.arange(peer_slots, dtype=jnp.int32) // PAGE
    fresh_valid = (slot_page[None, :] < count_from[:, None]).reshape(-1)
    mixed_local = attend_local(
        step_query[0],
        stored_keys[0],
        stored_values[0],
        jnp.take(context_tokens, device),
        fresh_keys,
        fresh_values,
        fresh_valid,
        step_key[0],
        step_value[0],
    ).reshape(1, -1)
    portion = lax.all_gather(mixed_local, "dev", axis=0, tiled=True)
    plain_result = jnp.dot(portion, output_matrix, preferred_element_type=jnp.float32)
    selected_output = selected_narrow(portion, adapter_down_output, request_adapter)
    partial_output = plain_result + adapter_scale * jnp.dot(
        selected_output, adapter_up_output.astype(jnp.float32), precision=lax.Precision.HIGHEST
    )
    return lax.psum(partial_output, "tp").astype(jnp.bfloat16)


def iota(shape, axis):
    return lax.broadcasted_iota(jnp.int32, shape, axis)


def dot32(a, b):
    return jnp.dot(a, b, preferred_element_type=jnp.float32)


def dot_rows(a, b):
    return lax.dot_general(a, b, (((1,), (1,)), ((), ())), preferred_element_type=jnp.float32)


def halves(value):
    high = value.astype(jnp.bfloat16)
    return high, (value - high.astype(jnp.float32)).astype(jnp.bfloat16)


def fused_kernel(
    devices,
    side,
    capacity,
    x_hbm,
    wk_hbm,
    wv_hbm,
    ad_hbm,
    upk_ref,
    upv_ref,
    adapter_ref,
    owner_ref,
    context_ref,
    query_ref,
    lastk_ref,
    lastv_ref,
    oldk_hbm,
    oldv_hbm,
    wo_hbm,
    ado_hbm,
    auo_hbm,
    out_ref,
    raw,
    acts,
    weights,
    upcat,
    token_owner,
    shipped,
    landed,
    sent,
    got,
    oldk,
    oldv,
    wo,
    ado,
    auo,
    mixes,
    part,
    other,
    local_sem,
    xs_sem,
    xr_sem,
    fs_sem,
    fr_sem,
    zs_sem,
    zr_sem,
    ys_sem,
    yr_sem,
    qs_sem,
    qr_sem,
    es_sem,
    er_sem,
    ps_sem,
    pr_sem,
    ms_sem,
    mr_sem,
    ts_sem,
    tr_sem,
):
    group = lax.axis_index("group")
    me = lax.axis_index("dev")
    core = lax.axis_index("tp")
    partner = (group, me, 1 - core)
    tok = x_hbm.shape[0]
    depth = wk_hbm.shape[0]
    width = wk_hbm.shape[1]
    low = ad_hbm.shape[1]
    half = tok // 2
    slots = capacity * PAGE
    outer = devices // side
    mz, mx = me // side, me % side
    beside = (group, mz * side + 1 - mx, core)
    across = (1 - group, me, core)
    kv_local = width // HEAD
    chunks = 1 + 2 * kv_local
    mesh_ids = pl.DeviceIdType.MESH

    def ahead(k):
        return ((mz + k // side) % outer) * side + (mx + k % side) % side

    def behind(k):
        return ((mz + outer - k // side) % outer) * side + (mx + side - k % side) % side

    def source_of(j):
        if j == 0:
            return ad_hbm, 0
        if j <= kv_local:
            return wk_hbm, (j - 1) * HEAD
        return wv_hbm, (j - 1 - kv_local) * HEAD

    def rows_of(j, cut):
        if j == 0:
            size = depth // 4
            return pl.ds(pl.multiple_of((cut * 2 + core) * size, size), size)
        size = depth // 2
        return pl.ds(pl.multiple_of(cut * size, size), size)

    def remote(src, dst, send, recv, device):
        return pltpu.make_async_remote_copy(
            src_ref=src,
            dst_ref=dst,
            send_sem=send,
            recv_sem=recv,
            device_id=device,
            device_id_type=mesh_ids,
        )

    own_half = pl.ds(pl.multiple_of(core * half, half), half)

    def columns(b, x):
        return pl.ds(pl.multiple_of((b * side + x) * depth, depth), depth)

    locals_ = []
    for j in range(chunks):
        ref, at = source_of(j)
        locals_.append(
            pltpu.make_async_copy(ref.at[:, pl.ds(at, HEAD)], weights.at[j, mz], local_sem.at[j])
        )
    for b in range(outer):
        locals_.append(
            pltpu.make_async_copy(
                x_hbm.at[:, columns(b, mx)], raw.at[0, b], local_sem.at[chunks + b]
            )
        )
    rest_at = chunks + outer
    later = [(oldk_hbm, oldk), (oldv_hbm, oldv), (wo_hbm, wo), (ado_hbm, ado), (auo_hbm, auo)]
    for i, (ref, to) in enumerate(later):
        locals_.append(pltpu.make_async_copy(ref, to, local_sem.at[rest_at + i]))

    barrier = pltpu.get_barrier_semaphore()
    for k in range(1, devices):
        pl.semaphore_signal(
            barrier, inc=1, device_id=(group, ahead(k), core), device_id_type=mesh_ids
        )
    pl.semaphore_signal(barrier, inc=1, device_id=partner, device_id_type=mesh_ids)
    pl.semaphore_signal(barrier, inc=1, device_id=across, device_id_type=mesh_ids)
    pl.semaphore_wait(barrier, devices + 1)

    def x_copy(b):
        return remote(
            x_hbm.at[own_half, columns(b, 1 - mx)],
            raw.at[1, b, own_half],
            xs_sem.at[b],
            xr_sem.at[b],
            beside,
        )

    def x_forward(b):
        view = raw.at[1, b, own_half]
        return remote(view, view, fs_sem.at[b], fr_sem.at[b], partner)

    def z_first(j, up):
        ref, at = source_of(j)
        to = mz + 1 if up else mz - 1
        return remote(
            ref.at[rows_of(j, group), pl.ds(at, HEAD)],
            weights.at[j, mz, rows_of(j, group)],
            zs_sem.at[j, mz, 0 if up else 1],
            zr_sem.at[j, mz],
            (group, to * side + mx, core),
        )

    def z_relay(j, b, up):
        view = weights.at[j, b, rows_of(j, group)]
        to = mz + 1 if up else mz - 1
        return remote(
            view,
            view,
            zs_sem.at[j, b, 0 if up else 1],
            zr_sem.at[j, b],
            (group, to * side + mx, core),
        )

    def y_copy(j, b):
        view = weights.at[j, b, rows_of(j, group)]
        return remote(view, view, ys_sem.at[j, b], yr_sem.at[j, b], across)

    def y_arrival(j, b):
        view = weights.at[j, b, rows_of(j, 1 - group)]
        return remote(view, view, ys_sem.at[j, b], yr_sem.at[j, b], across)

    def q_copy(b, cut, which):
        view = weights.at[0, b, rows_of(0, cut)]
        return remote(view, view, qs_sem.at[b, which], qr_sem.at[b, which], partner)

    def issue(j):
        @pl.when(mz < outer - 1)
        def _():
            z_first(j, True).start()

        @pl.when(mz > 0)
        def _():
            z_first(j, False).start()

    def relay(j):
        for t in range(1, outer):
            for up in (True, False):
                b = mz - t if up else mz + t

                @pl.when(b >= 0 if up else b < outer)
                def _():
                    z_relay(j, b, up).wait_recv()

                    @pl.when(mz < outer - 1 if up else mz > 0)
                    def _():
                        z_relay(j, b, up).start()

                    y_copy(j, b).start()
                    if j == 0:
                        q_copy(b, group, 0).start()

    def others(body):
        for t in range(1, outer):
            body((mz + t) % outer)

    def gather(j):
        if j == 0:

            def pass_on(b):
                y_arrival(0, b).wait_recv()
                q_copy(b, 1 - group, 1).start()

            def take(b):
                q_copy(b, group, 0).wait_recv()
                q_copy(b, 1 - group, 1).wait_recv()

            others(pass_on)
            others(take)
        else:
            others(lambda b: y_arrival(j, b).wait_recv())

    def part_copy(j, o):
        peer = ahead(o)
        return remote(
            sent.at[j, pl.ds(pl.multiple_of(peer * slots, slots), slots)],
            got.at[j, pl.ds(pl.multiple_of(me * slots, slots), slots)],
            ps_sem.at[j, o],
            pr_sem.at[j, o],
            (group, peer, core),
        )

    def part_arrival(j, o):
        peer = behind(o)
        return remote(
            sent.at[j, pl.ds(pl.multiple_of(peer * slots, slots), slots)],
            got.at[j, pl.ds(pl.multiple_of(peer * slots, slots), slots)],
            ps_sem.at[j, o],
            pr_sem.at[j, o],
            (group, peer, core),
        )

    def exchange(j):
        return remote(shipped.at[j], landed.at[j], es_sem.at[j], er_sem.at[j], beside)

    issue(0)
    issue(1)
    for b in range(outer):
        x_copy(b).start()
    for copy in locals_:
        copy.start()

    relay(0)
    issue(2)

    pages = owner_ref.shape[1]
    spread = (iota((pages, tok), 1) // PAGE == iota((pages, tok), 0)).astype(jnp.bfloat16)
    token_owner[...] = dot32(owner_ref[...].astype(jnp.float32).astype(jnp.bfloat16), spread)
    earlier = (iota((tok, tok), 0) // PAGE < iota((tok, tok), 1) // PAGE).astype(jnp.bfloat16)
    lora = low // 2
    fresh = devices * slots
    upcat[...] = jnp.zeros_like(upcat)
    upcat[pl.ds(0, lora), pl.ds(0, width)] = upk_ref[...]
    upcat[pl.ds(lora, lora), pl.ds(width, width)] = upv_ref[...]
    adapters = adapter_ref[...].astype(jnp.float32)
    slot_rows = devices * slots
    row_adapter = jnp.sum(
        jnp.where(iota((slot_rows, devices), 0) // slots == iota((slot_rows, devices), 1), adapters, 0.0),
        axis=1,
        keepdims=True,
    )
    low_adapter = ((iota((slot_rows, low), 1) % lora) // LOW_RANK).astype(jnp.float32)
    keep_low = low_adapter == row_adapter

    def mover(source):
        owners = token_owner[pl.ds(source, 1), :]
        hot = (iota((devices, tok), 0).astype(jnp.float32) == owners).astype(jnp.float32)
        before = dot32(hot.astype(jnp.bfloat16), earlier)
        rank = jnp.sum(before * hot, axis=0, keepdims=True)
        place = owners * float(slots) + rank + (iota((1, tok), 1) % PAGE).astype(jnp.float32)
        return (iota((fresh, tok), 0).astype(jnp.float32) == place).astype(jnp.bfloat16)

    row_owner = (iota((fresh, 1), 0) // slots).astype(jnp.float32)
    contexts = context_ref[...].astype(jnp.float32)
    start_at = jnp.sum(
        jnp.where(iota((fresh, devices), 0) // slots == iota((fresh, devices), 1), contexts, 0.0),
        axis=1,
        keepdims=True,
    )
    ahead_of = jnp.zeros((fresh, tok), jnp.float32)
    for block in range(devices):
        line = jnp.where(block < me, token_owner[block : block + 1, :], -1.0)
        ahead_of = ahead_of + (line == row_owner).astype(jnp.float32)
    position = (
        start_at
        + jnp.sum(ahead_of, axis=1, keepdims=True)
        + (iota((fresh, 1), 0) % slots).astype(jnp.float32)
    )
    half_size = HEAD // 2
    lane = iota((1, HEAD), 1)
    exponent = (lane % half_size).astype(jnp.float32) * (2.0 / HEAD)
    frequency = jnp.exp(-jnp.log(jnp.full((1, HEAD), rope_base, jnp.float32)) * exponent)
    angle = position * frequency
    cosine = jnp.cos(angle)
    sine = jnp.sin(angle)
    sine = jnp.where(lane < half_size, -sine, sine)

    own_move = mover(me)
    side_move = mover(mz * side + 1 - mx)
    relay(1)
    issue(3)
    for b in range(outer):
        locals_[chunks + b].wait()
        acts[0, b] = dot32(own_move, raw[0, b]).astype(jnp.bfloat16)
    relay(2)
    issue(4)
    gather(0)
    gather(1)
    for b in range(outer):
        x_copy(b).wait_recv()
        x_forward(b).start()
    for b in range(outer):
        x_forward(b).wait_recv()
        acts[1, b] = dot32(side_move, raw[1, b]).astype(jnp.bfloat16)
    for copy in locals_[:chunks]:
        copy.wait()

    def product(i, j):
        total = dot32(acts[i, 0], weights[j, 0])
        for b in range(1, outer):
            total = total + dot32(acts[i, b], weights[j, b])
        return total

    def multiply(j):
        shipped[j] = product(1, j)
        exchange(j).start()
        return product(0, j)

    def finish(j, own, low_parts):
        exchange(j).wait_recv()
        total = own + landed[j]
        at = (j - 1) * HEAD
        for piece in low_parts:
            total = total + dot32(piece, upcat[:, at : at + HEAD])
        if j <= kv_local:
            total = total * cosine + pltpu.roll(total, half_size, 1) * sine
        sent[j] = total.astype(jnp.bfloat16)
        for o in range(1, devices):
            part_copy(j, o).start()
        mine_at = pl.ds(pl.multiple_of(me * slots, slots), slots)
        got[j, mine_at, :] = sent[j, mine_at, :]

    own_low = multiply(0)
    own_1 = multiply(1)
    relay(3)
    gather(2)
    own_2 = multiply(2)
    gather(3)
    own_3 = multiply(3)
    exchange(0).wait_recv()
    low_parts = halves(jnp.where(keep_low, own_low + landed[0], 0.0))
    finish(1, own_1, low_parts)
    relay(4)
    gather(4)
    own_4 = multiply(4)
    finish(2, own_2, low_parts)
    finish(3, own_3, low_parts)

    mine = (token_owner[...] == me.astype(jnp.float32)).astype(jnp.float32)
    context = jnp.sum(
        jnp.where(iota((1, devices), 1) == me, context_ref[...].astype(jnp.float32), 0.0),
        axis=1,
        keepdims=True,
    )
    count = jnp.sum(mine, axis=1, keepdims=True)
    fresh_count = jnp.sum(
        jnp.where(iota((devices, fresh), 1) // slots == iota((devices, fresh), 0), count, 0.0),
        axis=0,
        keepdims=True,
    )
    fresh_valid = (iota((1, fresh), 1) % slots).astype(jnp.float32) < fresh_count
    for copy in locals_[rest_at:]:
        copy.wait()
    members = HEADS // KV_HEADS
    scale = HEAD ** (-0.5)
    query = query_ref[...].astype(jnp.float32)
    old_count = oldk.shape[0]
    old_valid = iota((1, old_count), 1).astype(jnp.float32) < context
    queries, old_scores, last_scores = [], [], []
    for h in range(kv_local):
        heads = jnp.concatenate(
            [query[:, (h * members + g) * HEAD : (h * members + g + 1) * HEAD] for g in range(members)],
            axis=0,
        )
        cols = slice(h * HEAD, (h + 1) * HEAD)
        queries.append(heads.astype(jnp.bfloat16))
        old_scores.append(
            jnp.where(old_valid, dot_rows(queries[h], oldk[:, cols]) * scale, -1e30)
        )
        last_scores.append(
            jnp.sum(heads * lastk_ref[:, cols].astype(jnp.float32), axis=1, keepdims=True) * scale
        )

    def settle(j):
        for o in range(1, devices):
            part_arrival(j, o).wait_recv()

    fresh_scores_of = []
    for h in range(kv_local):
        settle(1 + h)
        fresh_scores_of.append(
            jnp.where(fresh_valid, dot_rows(queries[h], got[1 + h]) * scale, -1e30)
        )
    finish(4, own_4, low_parts)
    for h in range(kv_local):
        cols = slice(h * HEAD, (h + 1) * HEAD)
        fresh_scores = fresh_scores_of[h]
        top = jnp.maximum(
            jnp.maximum(
                jnp.max(old_scores[h], axis=1, keepdims=True),
                jnp.max(fresh_scores, axis=1, keepdims=True),
            ),
            last_scores[h],
        )
        old_weights = jnp.exp(old_scores[h] - top)
        fresh_weights = jnp.exp(fresh_scores - top)
        last_weight = jnp.exp(last_scores[h] - top)
        total = (
            jnp.sum(old_weights, axis=1, keepdims=True)
            + jnp.sum(fresh_weights, axis=1, keepdims=True)
            + last_weight
        )
        settle(1 + kv_local + h)
        value = got[1 + kv_local + h]
        mixed = dot32((old_weights / total).astype(jnp.bfloat16), oldv[:, cols])
        mixed = mixed + dot32((fresh_weights / total).astype(jnp.bfloat16), value)
        mixed = mixed + (last_weight / total).astype(jnp.bfloat16).astype(jnp.float32) * lastv_ref[
            :, cols
        ].astype(jnp.float32)
        mixes[me, pl.ds(h * members, members), :] = mixed.astype(jnp.bfloat16).astype(jnp.float32)

    def mix_copy(o, row):
        return pltpu.make_async_remote_copy(
            src_ref=mixes.at[row],
            dst_ref=mixes.at[row],
            send_sem=ms_sem.at[o],
            recv_sem=mr_sem.at[o],
            device_id=(group, ahead(o), core),
            device_id_type=pl.DeviceIdType.MESH,
        )

    for o in range(1, devices):
        mix_copy(o, me).start()
    for o in range(1, devices):
        mix_copy(o, behind(o)).wait_recv()
    everyone = jnp.concatenate(
        [mixes[:, h, :] for h in range(kv_local * members)], axis=1
    ).astype(jnp.bfloat16)
    narrowed = dot_rows(everyone, ado[...])
    row_of = jnp.sum(
        jnp.where(iota((devices, devices), 0) == iota((devices, devices), 1), adapters, 0.0),
        axis=1,
        keepdims=True,
    )
    narrow_adapter = (
        (iota((devices, narrowed.shape[1]), 1) % (ADAPTER_COUNT * LOW_RANK)) // LOW_RANK
    ).astype(jnp.float32)
    high, rest = halves(jnp.where(narrow_adapter == row_of, narrowed, 0.0))
    part[...] = dot32(everyone, wo[...]) + dot32(high, auo[...]) + dot32(rest, auo[...])
    swap = pltpu.make_async_remote_copy(
        src_ref=part,
        dst_ref=other,
        send_sem=ts_sem,
        recv_sem=tr_sem,
        device_id=partner,
        device_id_type=pl.DeviceIdType.MESH,
    )
    swap.start()

    for b in range(outer):
        x_copy(b).wait_send()
        x_forward(b).wait_send()
    for o in range(1, devices):
        mix_copy(o, me).wait_send()
    for j in range(chunks):
        exchange(j).wait_send()
        if j > 0:
            for o in range(1, devices):
                part_copy(j, o).wait_send()

        @pl.when(mz < outer - 1)
        def _():
            z_first(j, True).wait_send()

        @pl.when(mz > 0)
        def _():
            z_first(j, False).wait_send()

        for t in range(1, outer):
            for up in (True, False):
                b = mz - t if up else mz + t

                @pl.when(b >= 0 if up else b < outer)
                def _():
                    @pl.when(mz < outer - 1 if up else mz > 0)
                    def _():
                        z_relay(j, b, up).wait_send()

                    y_copy(j, b).wait_send()
                    if j == 0:
                        q_copy(b, group, 0).wait_send()
                        q_copy(b, 1 - group, 1).wait_send()

    swap.wait()
    out_ref[...] = (part[...] + other[...]).astype(jnp.bfloat16)


def fused(
    side,
    prompt_activations,
    key_matrix,
    value_matrix,
    adapter_down_keyvalue,
    adapter_up_key,
    adapter_up_value,
    request_adapter,
    page_request,
    context_tokens,
    step_query,
    step_key,
    step_value,
    stored_keys,
    stored_values,
    output_matrix,
    adapter_down_output,
    adapter_up_output,
):
    devices = lax.axis_size("dev")
    tok, _ = prompt_activations.shape
    depth, width = key_matrix.shape
    low = adapter_down_keyvalue.shape[1]
    capacity = slots_of(tok // PAGE, devices)
    slots = capacity * PAGE
    rows = request_adapter.shape[0]
    heads = step_query.shape[1] // HEAD
    outer = devices // side
    chunks = 1 + 2 * (width // HEAD)
    fresh = devices * slots
    out_width = output_matrix.shape[1]
    bf16, f32 = jnp.bfloat16, jnp.float32
    whole = pl.BlockSpec(memory_space=pltpu.VMEM)
    far = pl.BlockSpec(memory_space=pl.ANY)
    dma = pltpu.SemaphoreType.DMA
    return pl.pallas_call(
        functools.partial(fused_kernel, devices, side, capacity),
        out_shape=jax.ShapeDtypeStruct((rows, out_width), bf16),
        in_specs=[far] * 4 + [whole] * 8 + [far] * 5,
        out_specs=whole,
        scratch_shapes=[
            pltpu.VMEM((2, outer, tok, depth), bf16),
            pltpu.VMEM((2, outer, tok, depth), bf16),
            pltpu.VMEM((chunks, outer, depth, HEAD), bf16),
            pltpu.VMEM((low, 2 * width), bf16),
            pltpu.VMEM((devices, tok), f32),
            pltpu.VMEM((chunks, fresh, HEAD), f32),
            pltpu.VMEM((chunks, fresh, HEAD), f32),
            pltpu.VMEM((chunks, fresh, HEAD), bf16),
            pltpu.VMEM((chunks, fresh, HEAD), bf16),
            pltpu.VMEM(stored_keys.shape[1:], bf16),
            pltpu.VMEM(stored_values.shape[1:], bf16),
            pltpu.VMEM(output_matrix.shape, bf16),
            pltpu.VMEM(adapter_down_output.shape[::-1], bf16),
            pltpu.VMEM(adapter_up_output.shape, bf16),
            pltpu.VMEM((devices, heads, HEAD), f32),
            pltpu.VMEM((rows, out_width), f32),
            pltpu.VMEM((rows, out_width), f32),
            dma((chunks + outer + 5,)),
            dma((outer,)),
            dma((outer,)),
            dma((outer,)),
            dma((outer,)),
            dma((chunks, outer, 2)),
            dma((chunks, outer)),
            dma((chunks, outer)),
            dma((chunks, outer)),
            dma((outer, 2)),
            dma((outer, 2)),
            dma((chunks,)),
            dma((chunks,)),
            dma((chunks, devices)),
            dma((chunks, devices)),
            dma((devices,)),
            dma((devices,)),
            dma,
            dma,
        ],
        compiler_params=pltpu.CompilerParams(
            collective_id=0, has_side_effects=True, vmem_limit_bytes=60 * 1024 * 1024
        ),
    )(
        prompt_activations,
        key_matrix,
        value_matrix,
        adapter_down_keyvalue,
        adapter_up_key,
        adapter_up_value,
        request_adapter.reshape(1, -1),
        page_request.reshape(devices, -1),
        context_tokens.reshape(1, -1),
        step_query,
        step_key,
        step_value,
        stored_keys[0],
        stored_values[0],
        output_matrix,
        adapter_down_output.T,
        adapter_up_output,
    )


def slots_of(pages_here, devices):
    return max(2, (pages_here + devices - 1) // devices)


def choose(*args):
    devices = lax.axis_size("dev")
    tok = args[0].shape[0]
    depth, width = args[1].shape
    slots = slots_of(tok // PAGE, devices) * PAGE
    fits = (
        lax.axis_size("tp") == 2
        and lax.axis_size("group") == 2
        and devices >= 4
        and args[6].shape[0] == devices
        and devices % 2 == 0
        and devices <= 16
        and devices * slots == tok
        and tok <= 256
        and depth % 128 == 0
        and width == 2 * HEAD
        and args[3].shape[1] == HEAD
        and slots % 16 == 0
    )
    if fits:
        return fused(2, *args)
    return per_device(*args)


def solution(mesh):
    return jax.shard_map(
        choose,
        mesh=mesh,
        in_specs=(
            P(("group", "dev"), None),
            P("dev", "tp"),
            P("dev", "tp"),
            P("dev", None),
            P(None, "tp"),
            P(None, "tp"),
            P("group"),
            P("group", None),
            P("group"),
            P(("group", "dev"), "tp"),
            P(("group", "dev"), "tp"),
            P(("group", "dev"), "tp"),
            P(("group", "dev"), None, "tp"),
            P(("group", "dev"), None, "tp"),
            P("tp", "dev"),
            P("tp", None),
            P(None, "dev"),
        ),
        out_specs=P("group", "dev"),
        check_vma=False,
    )
```
